32 devices in a mesh: group: 4 (over z), expert: 4 (over y, x), replica: 2 (over core).
Axes of the slice: x: 2, y: 2, z: 4, core: 2. Of those that a mesh axis runs over, the one named last changes fastest.
Arguments:
- cotangent: bfloat16 [1024, 2048], P(('group', 'expert')), may hold values from -6 to 6
- expert_ids: int32 [2, 1024, 4], P('replica', ('group', 'expert')), may hold values from 0 to 7, all different within a row; in each aligned block of 64 rows (0 to 63, 64 to 127, ..., all dimensions but the last counted through in order) at most 64 rows name the same one
- gate_probs: float32 [2, 1024, 4], P('replica', ('group', 'expert')), may hold values from 0.05 to 1
- saved_gate: bfloat16 [16, 2048, 384], P(('group', 'expert'), 'replica'), may hold values from -6 to 6
- saved_up: bfloat16 [16, 2048, 384], P(('group', 'expert'), 'replica'), may hold values from -6 to 6
- w_gate: bfloat16 [16, 2048, 384], P(('group', 'expert')), may hold values from -0.21875 to 0.21875
- w_up: bfloat16 [16, 2048, 384], P(('group', 'expert')), may hold values from -0.21875 to 0.21875
- w_down: bfloat16 [16, 384, 2048], P(('group', 'expert')), may hold values from -0.21875 to 0.21875
Outputs:
- grad_input: bfloat16 [1024, 2048], P(('group', 'expert'), 'replica')
- grad_down: float32 [16, 384, 2048], P(('group', 'expert'), None, 'replica')
The draws below stay inside these ranges and needn't reach their ends.
Inputs may be any that keep to these rules, and one draw needn't show every extreme that they name: `expert_ids`: each row of 4 entries names different experts. For each replica index and each block of 64 tokens no expert is named more than 64 times, and in every draw some expert is named exactly 64 times in some block.
All inputs are finite; a program needn't handle non-finite values.
Results may differ from the reference program's by a relative error of at most 0.0071.
Values may be sent and summed in bfloat16 or wider, within the bound.
A program may use at most 64 MiB of HBM per device.

```python
import math
import jax
import jax.numpy as jnp
import numpy as np
from jax import lax

D = 2048
FF = 768
TOK_DEV = 64
KREP = 4
EXPERTS = 8
UNITS = 16
FFH = 384
CAP = 64
SLOTS = 1024
TOKENS = 1024
N_GROUP = 4
N_EXPERT = 4
N_REPLICA = 2


def level_of(key, shape, pieces, low, largest):
    def one(position, shards_of):
        draws = jax.random.uniform(jax.random.fold_in(jax.random.fold_in(key, 6), position), (shards_of,), jnp.float32, low / len(pieces), largest / len(pieces))
        return jnp.repeat(jnp.exp(draws), shape[position] // shards_of).reshape((-1,) + (1,) * (len(shape) - position - 1))

    gain = one(*pieces[0])
    for cut in pieces[1:]:
        gain = gain * one(*cut)
    return gain


def shared_out(key, own, number, rows, number_of, top, limit, skew):
    order = jax.random.permutation(key, number_of)
    heavy_load, usual = load_shares(number_of, rows * top, limit, skew, True), load_shares(number_of, rows * top, limit, skew, False)
    places = jnp.arange(number_of)

    def named(lengths, rotation):
        used = int((lengths > 0).sum())
        fixed = max(1, used // 4)
        passed = fixed + (places - fixed + rotation * (used - fixed)) % max(1, number_of - fixed)
        return jnp.zeros((number_of,), jnp.int32).at[order[jnp.where(places < fixed, places, passed)]].set(jnp.asarray(lengths, jnp.int32))

    lengths = jnp.where(number % 4 == 0, named(heavy_load, number // 4), named(usual, number - number // 4 - 1))
    mixed = jax.random.permutation(jax.random.fold_in(own, 3), number_of)
    giver, sink = mixed[0:number_of // 2 * 2:2], mixed[1:number_of // 2 * 2:2]
    margin = jnp.minimum(lengths[giver] - 1, limit - lengths[sink]) // 2
    margin = jnp.where((giver == order[0]) | (sink == order[0]) | (lengths[sink] == 0), 0, jnp.maximum(margin, 0))
    passed = jax.random.randint(jax.random.fold_in(own, 4), (number_of // 2,), 0, 1 << 20) % (margin + 1)
    lengths = lengths.at[giver].add(-passed).at[sink].add(passed)
    items = jnp.searchsorted(jnp.cumsum(lengths), jnp.arange(rows * top), side="right").astype(jnp.int32)
    listing = items.reshape(top, rows).T
    listing = listing[jax.random.permutation(jax.random.fold_in(own, 1), rows)]
    rotation = jax.random.randint(jax.random.fold_in(own, 2), (rows, 1), 0, top)
    return jnp.take_along_axis(listing, (jnp.arange(top)[None, :] + rotation) % top, axis=1)


def load_shares(amount, total, most, lean, full):
    weights = [(1 << 20) // math.isqrt(standing ** lean) + 1 for standing in range(1, amount + 1)]
    largest = most if full else min(most, max(-(-total // amount), total * weights[0] // sum(weights)))
    least = 1 if total - largest >= amount - 1 else 0
    counts, spare = [largest] + [least] * (amount - 1), total - largest - least * (amount - 1)
    while spare > 0:
        candidates = [i for i in range(1, amount) if counts[i] < largest] or [i for i in range(1, amount) if counts[i] < most]
        whole, budget = sum([weights[i] for i in candidates]), spare
        for i in candidates:
            addition = min(most - counts[i], max(1, budget * weights[i] // whole), spare)
            counts[i] = counts[i] + addition
            spare = spare - addition
    return np.array(counts)


def scatter_about(key, dims, width, bound, shards=(), kind=jnp.bfloat16):
    drawn = jax.random.normal(key, dims, jnp.float32) * width
    if len(shards) > 0:
        drawn = level_of(key, dims, shards, -0.22, 0.18) * drawn
    return jnp.clip(drawn, min=-bound, max=bound).astype(kind)


def setup_inputs(seed: int = 0) -> dict:
    splits = jax.random.split(jax.random.key(seed), 9)
    cotangent = scatter_about(splits[0], (TOKENS, D), 1.0, 6.0, ((0, 16),))
    expert_ids_keys = jax.random.split(jax.random.fold_in(splits[1], 1), N_REPLICA * TOKENS // TOK_DEV)
    expert_ids_turns = jax.random.permutation(jax.random.fold_in(splits[1], 3), N_REPLICA * TOKENS // TOK_DEV)
    expert_ids = jax.vmap(lambda own, number: shared_out(jax.random.fold_in(splits[1], 2), own, number, TOK_DEV, EXPERTS, KREP, CAP, 2))(expert_ids_keys, expert_ids_turns).reshape((N_REPLICA, TOKENS, KREP))
    gate_probs = jnp.clip(jnp.exp(math.log(1.0) - 2.9957323 * jax.random.uniform(splits[2], (N_REPLICA, TOKENS, KREP), jnp.float32) ** level_of(splits[2], (N_REPLICA, TOKENS, KREP), ((0, 2), (1, 16)), -0.2, 0.2)), 0.05, 1.0)
    saved_gate = scatter_about(splits[3], (UNITS, N_REPLICA * SLOTS, FFH), 1.0, 6.0, ((0, 16), (1, 2)))
    saved_up = scatter_about(splits[4], (UNITS, N_REPLICA * SLOTS, FFH), 1.0, 6.0, ((0, 16), (1, 2)))
    w_gate = scatter_about(splits[5], (UNITS, D, FFH), FF ** -0.5, 0.21875, ((0, 16),))
    w_up = scatter_about(splits[6], (UNITS, D, FFH), FF ** -0.5, 0.21875, ((0, 16),))
    w_down = scatter_about(splits[7], (UNITS, FFH, D), FF ** -0.5, 0.21875, ((0, 16),))
    return {"cotangent": cotangent, "expert_ids": expert_ids, "gate_probs": gate_probs, "saved_gate": saved_gate, "saved_up": saved_up, "w_gate": w_gate, "w_up": w_up, "w_down": w_down}


def slots_of(id_row):
    positions = jnp.arange(id_row.shape[0], dtype=jnp.int32)
    same_expert = (id_row[:, None] == id_row[None, :]) & (positions[None, :] < positions[:, None])
    return jnp.sum(same_expert.astype(jnp.int32), axis=1)


def reference(cotangent, expert_ids, gate_probs, saved_gate, saved_up, w_gate, w_up, w_down):
    ndev = N_GROUP * N_EXPERT
    blocks = N_REPLICA * ndev
    assigned = TOK_DEV * KREP
    flat_ids = expert_ids.reshape(blocks, assigned).astype(jnp.int32)
    slot_pos = jax.vmap(slots_of)(flat_ids)
    scaled = (gate_probs[:, :, :, None] * cotangent[None, :, None, :].astype(jnp.float32)).astype(jnp.bfloat16)
    scaled = scaled.reshape(blocks, assigned, D)
    target = flat_ids * CAP + slot_pos
    block_idx = jnp.arange(blocks, dtype=jnp.int32)[:, None]
    packed = jnp.zeros((blocks, EXPERTS * CAP, D), jnp.bfloat16).at[block_idx, target].set(scaled)
    packed = packed.reshape(N_REPLICA, ndev, EXPERTS, CAP, D)
    gate_w = w_gate.reshape(N_GROUP // 2, 2, N_EXPERT, D, FFH)
    up_w = w_up.reshape(N_GROUP // 2, 2, N_EXPERT, D, FFH)
    down_w = w_down.reshape(N_GROUP // 2, 2, N_EXPERT, FFH, D)
    gate_saved = saved_gate.reshape(N_GROUP // 2, 2, N_EXPERT, N_REPLICA, SLOTS, FFH)
    up_saved = saved_up.reshape(N_GROUP // 2, 2, N_EXPERT, N_REPLICA, SLOTS, FFH)

    def per_expert(expert):
        pair_idx = expert // N_EXPERT
        column = expert % N_EXPERT
        rows_dy = lax.dynamic_index_in_dim(packed, expert, axis=2, keepdims=False)
        rows_dy = rows_dy.reshape(N_REPLICA, SLOTS, D).astype(jnp.float32)
        partials = []
        grads = []
        for half_idx in range(2):
            pre_gate = gate_saved[pair_idx, half_idx, column].astype(jnp.float32)
            pre_up = up_saved[pair_idx, half_idx, column].astype(jnp.float32)
            sigmoid_gate = jax.nn.sigmoid(pre_gate)
            silu_gate = pre_gate * sigmoid_gate
            activation = (silu_gate * pre_up).astype(jnp.bfloat16).astype(jnp.float32)
            down_f = down_w[pair_idx, half_idx, column].astype(jnp.float32)
            d_act = jnp.einsum('rsd,fd->rsf', rows_dy, down_f)
            d_gate = (d_act * pre_up * sigmoid_gate * (1.0 + pre_gate * (1.0 - sigmoid_gate))).astype(jnp.bfloat16)
            d_up = (d_act * silu_gate).astype(jnp.bfloat16)
            partial_value = jnp.einsum('rsf,df->rsd', d_gate.astype(jnp.float32), gate_w[pair_idx, half_idx, column].astype(jnp.float32))
            partial_value = partial_value + jnp.einsum('rsf,df->rsd', d_up.astype(jnp.float32), up_w[pair_idx, half_idx, column].astype(jnp.float32))
            partials.append(partial_value.astype(jnp.bfloat16).astype(jnp.float32))
            grad_terms = jnp.einsum('rsf,rsd->rfd', activation, rows_dy)
            grads.append(jnp.sum(grad_terms, axis=0))
        combined = (partials[0] + partials[1]).astype(jnp.bfloat16)
        return combined, jnp.stack(grads)

    combined_all, grads_all = lax.map(per_expert, jnp.arange(EXPERTS, dtype=jnp.int32))
    replica_of = (jnp.arange(blocks, dtype=jnp.int32) // ndev)[:, None]
    source_of = (jnp.arange(blocks, dtype=jnp.int32) % ndev)[:, None]
    gathered = combined_all[flat_ids, replica_of, source_of * CAP + slot_pos]
    gathered = gathered.reshape(N_REPLICA, ndev * TOK_DEV, KREP, D).astype(jnp.float32)
    grad_input = jnp.sum(gathered, axis=(0, 2)).astype(jnp.bfloat16)
    grad_down = grads_all.reshape(N_GROUP // 2, N_EXPERT, 2, FFH, D).transpose(0, 2, 1, 3, 4).reshape(UNITS, FFH, D)
    return grad_input, grad_down
```

```python
import functools

import jax
import jax.numpy as jnp
from jax import lax
from jax.experimental import pallas as pl
from jax.experimental.pallas import tpu as pltpu
from jax.sharding import PartitionSpec as P

MESH = pl.DeviceIdType.MESH
NT = (((1,), (1,)), ((), ()))


def from_partner(value, axis, bit):
    mask = 2**bit
    pairs = [(source, source ^ mask) for source in range(lax.axis_size(axis))]
    return lax.ppermute(value, axis, pairs)


def routed_plan(cotangent, expert_ids, gate_probs, saved_gate, saved_up, w_gate, w_up, w_down):
    n_group = lax.axis_size("group")
    n_expert = lax.axis_size("expert")
    tok_rows, model_width = cotangent.shape
    pick_count = expert_ids.shape[2]
    experts = n_group * n_expert // 2
    half_width = model_width // 2
    capacity = saved_gate.shape[1] // (n_group * n_expert)
    assigned = tok_rows * pick_count
    flat_ids = expert_ids.reshape(assigned)
    positions = jnp.arange(assigned, dtype=jnp.int32)
    same_expert = (flat_ids[:, None] == flat_ids[None, :]) & (
        positions[None, :] < positions[:, None]
    )
    slot_pos = jnp.sum(same_expert.astype(jnp.int32), axis=1)
    target = flat_ids * capacity + slot_pos
    places = jnp.arange(experts * capacity, dtype=jnp.int32)
    dispatch_map = (places[:, None] == target[None, :]).astype(jnp.bfloat16)
    scaled = (gate_probs[0][:, :, None] * cotangent[:, None, :].astype(jnp.float32)).astype(
        jnp.bfloat16
    )
    scaled = scaled.reshape(assigned, model_width)
    packed = jnp.dot(dispatch_map, scaled, preferred_element_type=jnp.float32).astype(jnp.bfloat16)
    packed = packed.reshape(n_group // 2, n_expert, capacity, 2, half_width)
    packed = packed.transpose(0, 3, 1, 2, 4).reshape(n_group, n_expert, capacity, half_width)
    arrived = lax.all_to_all(
        lax.all_to_all(packed, "expert", split_axis=1, concat_axis=1, tiled=True),
        "group",
        split_axis=0,
        concat_axis=0,
        tiled=True,
    )
    partner = from_partner(arrived, "group", 0)
    low_half = lax.axis_index("group") % 2 == 0
    front_half = jnp.where(low_half, arrived, partner)
    back_half = jnp.where(low_half, partner, arrived)
    dy_slots = jnp.concatenate([front_half, back_half], axis=3).reshape(-1, model_width)
    pre_gate = saved_gate[0].astype(jnp.float32)
    pre_up = saved_up[0].astype(jnp.float32)
    sigmoid_gate = jax.nn.sigmoid(pre_gate)
    silu_gate = pre_gate * sigmoid_gate
    activation = (silu_gate * pre_up).astype(jnp.bfloat16)
    d_act = lax.dot_general(
        dy_slots, w_down[0], (((1,), (1,)), ((), ())), preferred_element_type=jnp.float32
    )
    d_gate = (d_act * pre_up * sigmoid_gate * (1.0 + pre_gate * (1.0 - sigmoid_gate))).astype(
        jnp.bfloat16
    )
    d_up = (d_act * silu_gate).astype(jnp.bfloat16)
    partial_value = lax.dot_general(
        d_gate, w_gate[0], (((1,), (1,)), ((), ())), preferred_element_type=jnp.float32
    )
    partial_value = partial_value + lax.dot_general(
        d_up, w_up[0], (((1,), (1,)), ((), ())), preferred_element_type=jnp.float32
    )
    partial_value = partial_value.astype(jnp.bfloat16)
    own_half = jnp.where(low_half, partial_value[:, :half_width], partial_value[:, half_width:])
    peer_half = jnp.where(low_half, partial_value[:, half_width:], partial_value[:, :half_width])
    received = from_partner(peer_half, "group", 0)
    combined = (own_half.astype(jnp.float32) + received.astype(jnp.float32)).astype(jnp.bfloat16)
    combined = combined.reshape(n_group, n_expert, capacity, half_width)
    grad_terms = lax.dot_general(
        activation, dy_slots, (((0,), (0,)), ((), ())), preferred_element_type=jnp.float32
    )
    returned = lax.all_to_all(
        lax.all_to_all(combined, "group", split_axis=0, concat_axis=0, tiled=True),
        "expert",
        split_axis=1,
        concat_axis=1,
        tiled=True,
    )
    home_rows = returned.reshape(n_group // 2, 2, n_expert, capacity, half_width)
    home_rows = home_rows.transpose(0, 2, 3, 1, 4).reshape(experts * capacity, model_width)
    per_assign = lax.dot_general(
        dispatch_map, home_rows, (((0,), (0,)), ((), ())), preferred_element_type=jnp.float32
    )
    home_sum = jnp.sum(per_assign.reshape(tok_rows, pick_count, model_width), axis=1)
    grad_down, grad_input = (
        lax.psum_scatter(grad_terms, "replica", scatter_dimension=1, tiled=True),
        lax.psum_scatter(home_sum, "replica", scatter_dimension=1, tiled=True),
    )
    return (grad_input.astype(jnp.bfloat16), grad_down[None])


def dense_kernel(
    n_group,
    n_expert,
    cot_hbm,
    ids_ref,
    prob_ref,
    sg_hbm,
    su_hbm,
    wg_hbm,
    wu_hbm,
    wd_hbm,
    out_ref,
    gd_ref,
    gt_recv,
    sg_all,
    su_all,
    wg_ref,
    wu_ref,
    wd_ref,
    cot_all,
    meta_own,
    meta_give,
    meta_take,
    meta_z,
    meta_all,
    act_all,
    f_gate,
    f_up,
    p_buf,
    own0,
    rawr,
    r1,
    s2,
    r2,
    zs,
    zr,
    sibr,
    gt_send,
    ssem,
    rsem,
    lsem,
):
    tok, width = cot_hbm.shape
    ht = tok // 2
    half = width // 2
    raw_w = rawr.shape[-1]
    rows_g = n_expert * ht
    slots_g = n_expert * tok
    picks = ids_ref.shape[0]
    experts = meta_own.shape[0]
    f32, bf16 = jnp.float32, jnp.bfloat16
    g = lax.axis_index("group")
    ex = lax.axis_index("expert")
    r = lax.axis_index("replica")
    x, y = ex % 2, ex // 2
    nx, ny = 1 - x, 1 - y
    ex_x, ex_y, ex_d = y * 2 + nx, ny * 2 + x, ny * 2 + nx
    x_dev, y_dev, d_dev = (g, ex_x, r), (g, ex_y, r), (g, ex_d, r)
    sib_dev = (g, ex, 1 - r)

    def group_at(i):
        low = (g % 2 + i % 2) % 2
        high = (g // 2 + i // 2) % 2
        return low + 2 * high

    def z_dev(i, core=None):
        return (group_at(i), ex, r if core is None else core)

    number = {}
    started = []

    def copy(key, src, dst, dev):
        k = number.setdefault(key, len(number))
        return pltpu.make_async_remote_copy(
            src_ref=src,
            dst_ref=dst,
            send_sem=ssem.at[k],
            recv_sem=rsem.at[k],
            device_id=dev,
            device_id_type=MESH,
        )

    def send(key, src, dst, dev):
        one = copy(key, src, dst, dev)
        one.start()
        started.append(one)

    def recv(key, land, dev=sib_dev):
        copy(key, land, land, dev).wait_recv()

    def block(q, e, col, size):
        return cot_all.at[
            pl.ds(pl.multiple_of((q * n_expert + e) * ht, ht), ht), pl.ds(col, size)
        ]

    barrier = pltpu.get_barrier_semaphore()
    peers = [z_dev(i, core) for i in range(1, n_group) for core in (r, 1 - r)]
    peers += [x_dev, y_dev, d_dev, sib_dev]
    for dev in peers:
        pl.semaphore_signal(barrier, inc=1, device_id=dev, device_id_type=MESH)

    place = pltpu.make_async_copy(
        cot_hbm.at[pl.ds(pl.multiple_of(r * ht, ht), ht), :], block(g, ex, 0, width), lsem.at[0]
    )
    place.start()
    loads = [
        pltpu.make_async_copy(src, dst, lsem.at[1 + k])
        for k, (src, dst) in enumerate(
            [
                (sg_hbm.at[0], sg_all.at[r]),
                (su_hbm.at[0], su_all.at[r]),
                (wd_hbm.at[0], wd_ref),
                (wg_hbm.at[0], wg_ref),
                (wu_hbm.at[0], wu_ref),
            ]
        )
    ]
    for load in loads:
        load.start()

    named_by = lax.broadcasted_iota(jnp.int32, (experts, tok), 0)
    named = jnp.zeros((experts, tok), f32)
    weight = jnp.zeros((experts, tok), f32)
    for k in range(picks):
        same = ids_ref[k : k + 1, :] == named_by
        named = named + jnp.where(same, 1.0, 0.0)
        weight = weight + jnp.where(same, prob_ref[k : k + 1, :], 0.0)
    before = lax.broadcasted_iota(jnp.int32, (tok, tok), 0) < lax.broadcasted_iota(
        jnp.int32, (tok, tok), 1
    )
    slot = jnp.dot(
        named.astype(bf16), jnp.where(before, 1.0, 0.0).astype(bf16), preferred_element_type=f32
    )
    slot = jnp.where(named > 0.5, slot, -1.0)
    low_part = jnp.concatenate([slot[:, :ht], weight[:, :ht]], axis=1)
    high_part = jnp.concatenate([slot[:, ht:], weight[:, ht:]], axis=1)
    keep = jnp.where(r == 0, low_part, high_part)
    give = jnp.where(r == 0, high_part, low_part)
    blank = jnp.zeros((experts, tok), f32)

    def in_lanes(part):
        return jnp.concatenate(
            [jnp.where(r == 0, part, blank), jnp.where(r == 0, blank, part)], axis=1
        )

    keep, give = in_lanes(keep), in_lanes(give)
    for e in range(experts):
        meta_give[e] = give[e : e + 1, :]
    place.wait()
    pl.semaphore_wait(barrier, len(peers))

    def ag_cols(i, h):
        first = h * half + (raw_w if i == 1 else 0)
        size = ((half - raw_w) if i == 1 else half) // 2
        return (first, size), (first + size, size)

    def ag_own(i, h):
        a, b = (block(group_at(i), ex, *cols) for cols in ag_cols(i, h))
        send(("xa", i, h), a, a, x_dev)
        send(("yb", i, h), b, b, y_dev)
        send(("xb", i, h), b, b, x_dev)
        send(("ya", i, h), a, a, y_dev)

    def ag_forward(i, h):
        a, b = ag_cols(i, h)
        from_x, from_y = block(group_at(i), ex_x, *a), block(group_at(i), ex_y, *b)
        recv(("xa", i, h), from_x)
        send(("fa", i, h), from_x, from_x, y_dev)
        recv(("yb", i, h), from_y)
        send(("fb", i, h), from_y, from_y, x_dev)

    def ag_rest(i, h):
        a, b = ag_cols(i, h)
        recv(("xb", i, h), block(group_at(i), ex_x, *b))
        recv(("ya", i, h), block(group_at(i), ex_y, *a))

    def ag_corner(i, h):
        a, b = ag_cols(i, h)
        recv(("fa", i, h), block(group_at(i), ex_d, *a))
        recv(("fb", i, h), block(group_at(i), ex_d, *b))

    def z_out(i, h):
        mine = block(g, ex, h * half, half)
        send(("z", i, h), mine, mine, z_dev(i))

    def z_in(i, h):
        recv(("z", i, h), block(group_at(i), ex, h * half, half))

    def z_forward(h):
        there = block(group_at(3), ex, h * half, half)
        send(("z", 2, h), there, there, z_dev(1))

    def raw_out(e, name, h):
        there = block(g, e, h * half, raw_w)
        send(("raw", name, h), there, there, z_dev(1))

    def raw_in(h):
        for e, name in ((ex_x, "x"), (ex_y, "y"), (ex_d, "d")):
            recv(("raw", name, h), block(group_at(1), e, h * half, raw_w))

    send(("give",), meta_give, meta_take, sib_dev)
    z_out(3, 0)
    z_out(1, 0)
    ag_own(0, 0)
    send(("sg",), sg_hbm.at[0], sg_all.at[r], sib_dev)
    send(("su",), su_hbm.at[0], su_all.at[r], sib_dev)
    recv(("give",), meta_take)
    for e in range(experts):
        meta_own[e] = keep[e : e + 1, :] + meta_take[e]

    def experts_of(plane):
        return pl.ds((plane // 2) * n_expert, n_expert)

    def meta_spread(i):
        for key, e, dev in (("mx", ex_x, x_dev), ("my", ex_y, y_dev), ("md", ex_d, d_dev)):
            send((key, i), meta_z.at[i, e], meta_all.at[i, ex], dev)

    for i in (3, 1, 2):
        send(("mz", i), meta_own.at[experts_of(group_at(i))], meta_z.at[i], z_dev(i))
    meta_z[0] = meta_own[experts_of(g)]
    meta_spread(0)
    z_out(3, 1)
    z_out(1, 1)
    ag_own(0, 1)

    eye = lax.broadcasted_iota(jnp.int32, (2 * tok, 2 * tok), 0) == lax.broadcasted_iota(
        jnp.int32, (2 * tok, 2 * tok), 1
    )
    place_lane = lax.broadcasted_iota(jnp.int32, (ht, slots_g), 1).astype(f32)

    def rows_of(i):
        return pl.ds(pl.multiple_of(group_at(i) * rows_g, rows_g), rows_g)

    def factors(i):
        for key, e in (("mx", ex_x), ("my", ex_y), ("md", ex_d)):
            recv((key, i), meta_all.at[i, e])
        meta_all[i, ex] = meta_z[i, ex]
        columns = []
        for b in range(n_expert):
            columns.append(jnp.sum(jnp.where(eye, meta_all[i, b], 0.0), axis=1, keepdims=True))
        slots = pl.ds(pl.multiple_of(group_at(i) * slots_g, slots_g), slots_g)
        to_gate = to_up = to_act = None
        for rho in range(2):
            picked, weights = [], []
            for b in range(n_expert):
                spot = columns[b][rho * tok : rho * tok + ht]
                spot = jnp.where(spot < -0.5, -1.0, spot + float(b * tok))
                picked.append(jnp.where(place_lane == spot, 1.0, 0.0))
                weights.append(columns[b][rho * tok + ht : (rho + 1) * tok])
            select = jnp.concatenate(picked, axis=0).astype(bf16)
            weights = jnp.concatenate(weights, axis=0)
            gate = jnp.dot(select, sg_all[rho, slots, :], preferred_element_type=f32)
            up = jnp.dot(select, su_all[rho, slots, :], preferred_element_type=f32)
            sig = jax.nn.sigmoid(gate)
            silu = gate * sig
            of_up = weights * silu
            of_act = of_up * up
            of_gate = weights * up * sig * (1.0 + gate * (1.0 - sig))
            to_gate = of_gate if rho == 0 else to_gate + of_gate
            to_up = of_up if rho == 0 else to_up + of_up
            to_act = of_act if rho == 0 else to_act + of_act
        f_gate[i] = to_gate
        f_up[i] = to_up
        act_all[rows_of(i), :] = to_act.astype(bf16)

    def hidden_grads(i):
        d_act = lax.dot_general(
            cot_all[rows_of(i), :], wd_ref[...], NT, preferred_element_type=f32
        )
        return (d_act * f_gate[i]).astype(bf16), (d_act * f_up[i]).astype(bf16)

    def partial_of(grads, f):
        first = (1 - r if f == 0 else r) * half
        wide = pl.ds(pl.multiple_of(first, half), half)
        value = lax.dot_general(grads[0], wg_ref[wide, :], NT, preferred_element_type=f32)
        value = value + lax.dot_general(
            grads[1], wu_ref[wide, :], NT, preferred_element_type=f32
        )
        return value.reshape(2, 2, ht, half)

    def rs_cols(i, part):
        first, size = (0, half)
        if part == "raw":
            first, size = 0, raw_w
        if part == "rest":
            first, size = raw_w, half - raw_w
        return pl.ds(first, size // 2), pl.ds(first + size // 2, size // 2), pl.ds(first, size)

    def rs_first(i, f, part):
        a, b, _ = rs_cols(i, part)
        send(("a1", i, f, part), p_buf.at[i, f, ny, :, :, a], r1.at[i, f, :, :, a], y_dev)
        send(("b1", i, f, part), p_buf.at[i, f, :, nx, :, b], r1.at[i, f, :, :, b], x_dev)

    def rs_second(i, f, part):
        a, b, _ = rs_cols(i, part)
        recv(("a1", i, f, part), r1.at[i, f, :, :, a])
        left = p_buf[i, f, y, :, :, a].astype(f32) + r1[i, f, :, :, a].astype(f32)
        s2[i, f, :, :, a] = left.astype(bf16)
        send(("a2", i, f, part), s2.at[i, f, nx, :, a], r2.at[i, f, :, a], x_dev)
        recv(("b1", i, f, part), r1.at[i, f, :, :, b])
        right = p_buf[i, f, :, x, :, b].astype(f32) + r1[i, f, :, :, b].astype(f32)
        s2[i, f, :, :, b] = right.astype(bf16)
        send(("b2", i, f, part), s2.at[i, f, ny, :, b], r2.at[i, f, :, b], y_dev)

    def rs_third(i, f, part):
        a, b, both = rs_cols(i, part)
        recv(("a2", i, f, part), r2.at[i, f, :, a])
        left = s2[i, f, x, :, a].astype(f32) + r2[i, f, :, a].astype(f32)
        zs[i, f, :, a] = left.astype(bf16)
        recv(("b2", i, f, part), r2.at[i, f, :, b])
        right = s2[i, f, y, :, b].astype(f32) + r2[i, f, :, b].astype(f32)
        zs[i, f, :, b] = right.astype(bf16)
        if i > 0:
            send(
                ("home", i, f),
                zs.at[i, f, :, both],
                zr.at[i, f, :, both],
                z_dev(i, 1 - r if f == 0 else r),
            )

    def grad_chunk(j):
        base = (1 - r if j < 2 else r) * half + (j % 2) * (half // 2)
        cols = pl.ds(pl.multiple_of(base, half // 2), half // 2)
        value = lax.dot_general(
            act_all[...], cot_all[:, cols], (((0,), (0,)), ((), ())), preferred_element_type=f32
        )
        land = pl.ds((j % 2) * (half // 2), half // 2)
        if j < 2:
            gt_send[:, land] = value.astype(bf16)
        else:
            gd_ref[:, land] = value
        if j == 1:
            send(("grad",), gt_send, gt_recv, sib_dev)

    ag_forward(0, 0)
    ag_rest(0, 0)
    raw_out(ex_x, "x", 0)
    raw_out(ex_y, "y", 0)
    for i in (1, 3, 2):
        recv(("mz", i), meta_z.at[i])
        meta_spread(i)
    z_in(1, 0)
    ag_own(1, 0)
    ag_forward(0, 1)
    z_in(3, 0)
    z_forward(0)
    ag_own(3, 0)
    z_in(1, 1)
    ag_own(1, 1)
    ag_rest(0, 1)
    raw_out(ex_x, "x", 1)
    raw_out(ex_y, "y", 1)
    ag_corner(0, 0)
    raw_out(ex_d, "d", 0)
    for load in loads[:2]:
        load.wait()
    recv(("sg",), sg_all.at[1 - r])
    recv(("su",), su_all.at[1 - r])
    factors(0)
    ag_forward(1, 0)
    ag_corner(0, 1)
    raw_out(ex_d, "d", 1)
    z_in(3, 1)
    z_forward(1)
    ag_own(3, 1)
    ag_forward(1, 1)
    ag_forward(3, 0)
    loads[2].wait()
    grads = hidden_grads(0)
    z_in(2, 0)
    ag_own(2, 0)
    for load in loads[3:]:
        load.wait()
    for f in range(2):
        value = partial_of(grads, f)
        own0[f] = value[:, :, :, :raw_w]
        p_buf[0, f, :, :, :, pl.ds(raw_w, half - raw_w)] = value[:, :, :, raw_w:].astype(bf16)
    ag_forward(3, 1)
    z_in(2, 1)
    ag_own(2, 1)
    factors(3)
    ag_forward(2, 0)
    factors(1)
    ag_forward(2, 1)
    ag_rest(3, 0)
    ag_rest(3, 1)
    ag_corner(3, 0)
    ag_corner(3, 1)
    grads = hidden_grads(3)
    for f in range(2):
        p_buf[3, f] = partial_of(grads, f).astype(bf16)
        rs_first(3, f, "all")
    ag_rest(1, 0)
    ag_rest(1, 1)
    ag_corner(1, 0)
    ag_corner(1, 1)
    raw_in(0)
    raw_in(1)
    grads = hidden_grads(1)
    for f in range(2):
        p_buf[1, f] = partial_of(grads, f).astype(bf16)
        send(("merge", f), p_buf.at[1, f, :, :, :, pl.ds(0, raw_w)], rawr.at[f], z_dev(1))
    factors(2)
    rs_second(3, 0, "all")
    rs_second(3, 1, "all")
    ag_rest(2, 0)
    ag_rest(2, 1)
    ag_corner(2, 0)
    ag_corner(2, 1)
    grads = hidden_grads(2)
    for f in range(2):
        p_buf[2, f] = partial_of(grads, f).astype(bf16)
        rs_first(2, f, "all")
    rs_third(3, 0, "all")
    rs_third(3, 1, "all")
    for f in range(2):
        rs_first(1, f, "rest")
    for f in range(2):
        rs_first(0, f, "rest")
    grad_chunk(0)
    rs_second(2, 0, "all")
    grad_chunk(1)
    rs_second(2, 1, "all")
    for f in range(2):
        recv(("merge", f), rawr.at[f])
        value = own0[f] + rawr[f].astype(f32)
        p_buf[0, f, :, :, :, pl.ds(0, raw_w)] = value.astype(bf16)
        rs_first(0, f, "raw")
    rs_second(1, 0, "rest")
    rs_second(1, 1, "rest")
    rs_third(2, 0, "all")
    grad_chunk(2)
    rs_third(2, 1, "all")
    rs_second(0, 0, "rest")
    rs_second(0, 1, "rest")
    rs_third(1, 0, "rest")
    rs_third(1, 1, "rest")
    grad_chunk(3)
    rs_second(0, 0, "raw")
    rs_second(0, 1, "raw")
    rs_third(0, 0, "rest")
    rs_third(0, 0, "raw")
    send(("corner",), zs.at[0, 0], sibr, sib_dev)
    rs_third(0, 1, "rest")
    rs_third(0, 1, "raw")

    front, back = pl.ds(0, raw_w), pl.ds(raw_w, half - raw_w)

    def finish(own, f, rows):
        for i, cols in ((3, pl.ds(0, half)), (1, back), (2, pl.ds(0, half))):
            recv(("home", i, f), zr.at[i, f, :, cols])
        if f == 0:
            recv(("corner",), sibr)
        for cols in (front, back):
            total = own[:, cols].astype(f32)
            for i in (3, 2) if cols is front else (3, 1, 2):
                total = total + zr[i, f, :, cols].astype(f32)
            out_ref[rows, cols] = total.astype(bf16)

    finish(zs.at[0, 1], 1, pl.ds(pl.multiple_of(r * ht, ht), ht))
    finish(sibr, 0, pl.ds(pl.multiple_of((1 - r) * ht, ht), ht))
    recv(("grad",), gt_recv)
    for one in started:
        one.wait_send()


def finish_kernel(rows_ref, own_ref, other_ref, out_ref, gd_ref):
    out_ref[...] = rows_ref[...]
    gd_ref[0] = own_ref[...] + other_ref[...].astype(jnp.float32)


def dense_plan(cotangent, expert_ids, gate_probs, saved_gate, saved_up, w_gate, w_up, w_down):
    n_group = lax.axis_size("group")
    n_expert = lax.axis_size("expert")
    tok, width = cotangent.shape
    half, quarter = width // 2, width // 4
    hidden = w_down.shape[1]
    experts = n_group * n_expert // 2
    blocks = n_group * n_expert
    rows_g = n_expert * tok // 2
    bf16, f32 = jnp.bfloat16, jnp.float32
    vmem = pl.BlockSpec(memory_space=pltpu.VMEM)
    ht = tok // 2
    raw_w = quarter
    copies = 128
    cotangent, saved_gate, saved_up, w_gate, w_up, w_down = (
        pltpu.with_memory_space_constraint(value, pltpu.HBM)
        for value in (cotangent, saved_gate, saved_up, w_gate, w_up, w_down)
    )
    ids, probs = (
        pltpu.with_memory_space_constraint(value[0].T, pltpu.HBM)
        for value in (expert_ids, gate_probs)
    )
    here = pl.BlockSpec(memory_space=pltpu.HBM)
    rows, own, other = pl.pallas_call(
        functools.partial(dense_kernel, n_group, n_expert),
        out_shape=(
            jax.ShapeDtypeStruct((tok, half), bf16),
            jax.ShapeDtypeStruct((hidden, half), f32),
            jax.ShapeDtypeStruct((hidden, half), bf16),
        ),
        in_specs=[here, vmem, vmem] + [here] * 5,
        out_specs=(vmem, vmem, vmem),
        scratch_shapes=[
            pltpu.VMEM((2,) + saved_gate.shape[1:], bf16),
            pltpu.VMEM((2,) + saved_up.shape[1:], bf16),
            pltpu.VMEM(w_gate.shape[1:], bf16),
            pltpu.VMEM(w_up.shape[1:], bf16),
            pltpu.VMEM(w_down.shape[1:], bf16),
            pltpu.VMEM((blocks * ht, width), bf16),
            pltpu.VMEM((experts, 1, 2 * tok), f32),
            pltpu.VMEM((experts, 1, 2 * tok), f32),
            pltpu.VMEM((experts, 1, 2 * tok), f32),
            pltpu.VMEM((n_group, n_expert, 1, 2 * tok), f32),
            pltpu.VMEM((n_group, n_expert, 1, 2 * tok), f32),
            pltpu.VMEM((blocks * ht, hidden), bf16),
            pltpu.VMEM((n_group, rows_g, hidden), f32),
            pltpu.VMEM((n_group, rows_g, hidden), f32),
            pltpu.VMEM((n_group, 2, 2, 2, ht, half), bf16),
            pltpu.VMEM((2, 2, 2, ht, raw_w), f32),
            pltpu.VMEM((2, 2, 2, ht, raw_w), bf16),
            pltpu.VMEM((n_group, 2, 2, ht, half), bf16),
            pltpu.VMEM((n_group, 2, 2, ht, half), bf16),
            pltpu.VMEM((n_group, 2, ht, half), bf16),
            pltpu.VMEM((n_group, 2, ht, half), bf16),
            pltpu.VMEM((n_group, 2, ht, half), bf16),
            pltpu.VMEM((ht, half), bf16),
            pltpu.VMEM((hidden, half), bf16),
            pltpu.SemaphoreType.DMA((copies,)),
            pltpu.SemaphoreType.DMA((copies,)),
            pltpu.SemaphoreType.DMA((6,)),
        ],
        compiler_params=pltpu.CompilerParams(
            collective_id=0, has_side_effects=True, vmem_limit_bytes=40 * 1024 * 1024
        ),
    )(
        cotangent,
        ids,
        probs,
        saved_gate,
        saved_up,
        w_gate,
        w_up,
        w_down,
    )
    return pl.pallas_call(
        finish_kernel,
        out_shape=(
            jax.ShapeDtypeStruct((tok, half), bf16),
            jax.ShapeDtypeStruct((1, hidden, half), f32),
        ),
        in_specs=[vmem] * 3,
        out_specs=(vmem, vmem),
        compiler_params=pltpu.CompilerParams(vmem_limit_bytes=8 * 1024 * 1024),
    )(rows, own, other)


def on_device(cotangent, expert_ids, gate_probs, saved_gate, saved_up, w_gate, w_up, w_down):
    n_group = lax.axis_size("group")
    n_expert = lax.axis_size("expert")
    n_replica = lax.axis_size("replica")
    tok_rows = cotangent.shape[0]
    capacity = saved_gate.shape[1] // (n_group * n_expert)
    small = n_group == 4 and n_expert == 4 and n_replica == 2
    plan = routed_plan
    if small and capacity == tok_rows and 2 * tok_rows == 128:
        plan = dense_plan
    return plan(cotangent, expert_ids, gate_probs, saved_gate, saved_up, w_gate, w_up, w_down)


def solution(mesh):
    return jax.shard_map(
        on_device,
        mesh=mesh,
        in_specs=(
            P(("group", "expert"), None),
            P("replica", ("group", "expert"), None),
            P("replica", ("group", "expert"), None),
            P(("group", "expert"), "replica", None),
            P(("group", "expert"), "replica", None),
            P(("group", "expert"), None, None),
            P(("group", "expert"), None, None),
            P(("group", "expert"), None, None),
        ),
        out_specs=(P(("group", "expert"), "replica"), P(("group", "expert"), None, "replica")),
        check_vma=False,
    )
```

```python
import functools

import jax
import jax.numpy as jnp
from jax import lax
from jax.experimental import pallas as pl
from jax.experimental.pallas import tpu as pltpu
from jax.sharding import PartitionSpec as P

MESH = pl.DeviceIdType.MESH
NT = (((1,), (1,)), ((), ()))


def from_partner(value, axis, bit):
    mask = 2**bit
    pairs = [(source, source ^ mask) for source in range(lax.axis_size(axis))]
    return lax.ppermute(value, axis, pairs)


def routed_plan(cotangent, expert_ids, gate_probs, saved_gate, saved_up, w_gate, w_up, w_down):
    n_group = lax.axis_size("group")
    n_expert = lax.axis_size("expert")
    tok_rows, model_width = cotangent.shape
    pick_count = expert_ids.shape[2]
    experts = n_group * n_expert // 2
    half_width = model_width // 2
    capacity = saved_gate.shape[1] // (n_group * n_expert)
    assigned = tok_rows * pick_count
    flat_ids = expert_ids.reshape(assigned)
    positions = jnp.arange(assigned, dtype=jnp.int32)
    same_expert = (flat_ids[:, None] == flat_ids[None, :]) & (
        positions[None, :] < positions[:, None]
    )
    slot_pos = jnp.sum(same_expert.astype(jnp.int32), axis=1)
    target = flat_ids * capacity + slot_pos
    places = jnp.arange(experts * capacity, dtype=jnp.int32)
    dispatch_map = (places[:, None] == target[None, :]).astype(jnp.bfloat16)
    scaled = (gate_probs[0][:, :, None] * cotangent[:, None, :].astype(jnp.float32)).astype(
        jnp.bfloat16
    )
    scaled = scaled.reshape(assigned, model_width)
    packed = jnp.dot(dispatch_map, scaled, preferred_element_type=jnp.float32).astype(jnp.bfloat16)
    packed = packed.reshape(n_group // 2, n_expert, capacity, 2, half_width)
    packed = packed.transpose(0, 3, 1, 2, 4).reshape(n_group, n_expert, capacity, half_width)
    arrived = lax.all_to_all(
        lax.all_to_all(packed, "expert", split_axis=1, concat_axis=1, tiled=True),
        "group",
        split_axis=0,
        concat_axis=0,
        tiled=True,
    )
    partner = from_partner(arrived, "group", 0)
    low_half = lax.axis_index("group") % 2 == 0
    front_half = jnp.where(low_half, arrived, partner)
    back_half = jnp.where(low_half, partner, arrived)
    dy_slots = jnp.concatenate([front_half, back_half], axis=3).reshape(-1, model_width)
    pre_gate = saved_gate[0].astype(jnp.float32)
    pre_up = saved_up[0].astype(jnp.float32)
    sigmoid_gate = jax.nn.sigmoid(pre_gate)
    silu_gate = pre_gate * sigmoid_gate
    activation = (silu_gate * pre_up).astype(jnp.bfloat16)
    d_act = lax.dot_general(
        dy_slots, w_down[0], (((1,), (1,)), ((), ())), preferred_element_type=jnp.float32
    )
    d_gate = (d_act * pre_up * sigmoid_gate * (1.0 + pre_gate * (1.0 - sigmoid_gate))).astype(
        jnp.bfloat16
    )
    d_up = (d_act * silu_gate).astype(jnp.bfloat16)
    partial_value = lax.dot_general(
        d_gate, w_gate[0], (((1,), (1,)), ((), ())), preferred_element_type=jnp.float32
    )
    partial_value = partial_value + lax.dot_general(
        d_up, w_up[0], (((1,), (1,)), ((), ())), preferred_element_type=jnp.float32
    )
    partial_value = partial_value.astype(jnp.bfloat16)
    own_half = jnp.where(low_half, partial_value[:, :half_width], partial_value[:, half_width:])
    peer_half = jnp.where(low_half, partial_value[:, half_width:], partial_value[:, :half_width])
    received = from_partner(peer_half, "group", 0)
    combined = (own_half.astype(jnp.float32) + received.astype(jnp.float32)).astype(jnp.bfloat16)
    combined = combined.reshape(n_group, n_expert, capacity, half_width)
    grad_terms = lax.dot_general(
        activation, dy_slots, (((0,), (0,)), ((), ())), preferred_element_type=jnp.float32
    )
    returned = lax.all_to_all(
        lax.all_to_all(combined, "group", split_axis=0, concat_axis=0, tiled=True),
        "expert",
        split_axis=1,
        concat_axis=1,
        tiled=True,
    )
    home_rows = returned.reshape(n_group // 2, 2, n_expert, capacity, half_width)
    home_rows = home_rows.transpose(0, 2, 3, 1, 4).reshape(experts * capacity, model_width)
    per_assign = lax.dot_general(
        dispatch_map, home_rows, (((0,), (0,)), ((), ())), preferred_element_type=jnp.float32
    )
    home_sum = jnp.sum(per_assign.reshape(tok_rows, pick_count, model_width), axis=1)
    grad_down, grad_input = (
        lax.psum_scatter(grad_terms, "replica", scatter_dimension=1, tiled=True),
        lax.psum_scatter(home_sum, "replica", scatter_dimension=1, tiled=True),
    )
    return (grad_input.astype(jnp.bfloat16), grad_down[None])


SCHEDULE = (
    ("zo", 3, 0), ("own", 0, 0), ("saved",), ("metaz",), ("zo", 1, 0), ("zo", 3, 1),
    ("own", 0, 1), ("meta", 0), ("fwa", 0, 0), ("fwb", 0, 0), ("own", 3, 0), ("zo", 1, 1),
    ("fwa", 0, 1), ("meta", 1), ("fwb", 0, 1), ("meta", 3), ("own", 1, 0), ("own", 3, 1),
    ("fwb", 3, 0), ("fwa", 3, 0), ("raw", "y", 1), ("fac", 0), ("raw", "x", 1), ("raw", "x", 0),
    ("raw", "d", 1), ("own", 2, 0), ("hid", 0), ("par", 0, 1), ("own", 1, 1), ("fwb", 3, 1),
    ("fwb", 1, 0), ("fwa", 3, 1), ("own", 2, 1), ("raw", "y", 0), ("fac", 3), ("raw", "d", 0),
    ("fac", 1), ("fwa", 1, 0), ("meta", 2), ("par", 0, 0), ("fwb", 1, 1), ("fwb", 2, 0),
    ("fwa", 1, 1), ("fwa", 2, 0), ("rs1", 0, 0, "rest"), ("hid", 3), ("par", 3, 0),
    ("fwb", 2, 1), ("fwa", 2, 1), ("par", 3, 1), ("hid", 1), ("par", 1, 0), ("par", 1, 1),
    ("rs1", 1, 1, "rest"), ("rs1", 0, 1, "rest"), ("fac", 2), ("rs2", 3, 0, "all"),
    ("rs1", 1, 0, "rest"), ("hid", 2), ("par", 2, 0), ("rs2", 3, 1, "all"), ("grad", 0),
    ("par", 2, 1), ("grad", 1), ("rs3", 3, 0, "all"), ("rs2", 1, 0, "rest"),
    ("rs2", 0, 1, "rest"), ("grad", 2), ("rs2", 2, 0, "all"), ("mrg", 0), ("rs3", 3, 1, "all"),
    ("rs2", 1, 1, "rest"), ("mrg", 1), ("rs2", 2, 1, "all"), ("rs3", 2, 0, "all"),
    ("rs2", 0, 0, "raw"), ("rs3", 1, 1, "rest"), ("rs2", 0, 0, "rest"), ("rs3", 1, 0, "rest"),
    ("rs3", 2, 1, "all"), ("grad", 3), ("rs3", 0, 1, "rest"), ("rs2", 0, 1, "raw"),
    ("rs3", 0, 0, "rest"), ("drain",), ("rs3", 0, 0, "raw"), ("corner",), ("rs3", 0, 1, "raw"),
)


def dense_kernel(
    n_group,
    n_expert,
    cot_hbm,
    ids_ref,
    prob_ref,
    sg_hbm,
    su_hbm,
    wg_hbm,
    wu_hbm,
    wd_hbm,
    out_ref,
    gd_ref,
    sg_all,
    su_all,
    wg_ref,
    wu_ref,
    wd_ref,
    cot_all,
    meta_own,
    meta_give,
    meta_take,
    meta_z,
    meta_all,
    act_all,
    f_gate,
    f_up,
    p_buf,
    own0,
    rawr,
    r1,
    s2,
    r2,
    zs,
    zr,
    sibr,
    gt_send,
    gt_recv,
    ssem,
    rsem,
    lsem,
):
    tok, width = cot_hbm.shape
    ht = tok // 2
    half = width // 2
    raw_w = rawr.shape[-1]
    rows_g = n_expert * ht
    slots_g = n_expert * tok
    picks = ids_ref.shape[0]
    experts = meta_own.shape[0]
    f32, bf16 = jnp.float32, jnp.bfloat16
    g = lax.axis_index("group")
    ex = lax.axis_index("expert")
    r = lax.axis_index("replica")
    x, y = ex % 2, ex // 2
    nx, ny = 1 - x, 1 - y
    ex_x, ex_y, ex_d = y * 2 + nx, ny * 2 + x, ny * 2 + nx
    x_dev, y_dev, d_dev = (g, ex_x, r), (g, ex_y, r), (g, ex_d, r)
    sib_dev = (g, ex, 1 - r)

    def group_at(i):
        low = (g % 2 + i % 2) % 2
        high = (g // 2 + i // 2) % 2
        return low + 2 * high

    def z_dev(i, core=None):
        return (group_at(i), ex, r if core is None else core)

    number = {}
    started, arrived, present = [], set(), set()

    def copy(key, src, dst, dev):
        k = number.setdefault(key, len(number))
        return pltpu.make_async_remote_copy(
            src_ref=src,
            dst_ref=dst,
            send_sem=ssem.at[k],
            recv_sem=rsem.at[k],
            device_id=dev,
            device_id_type=MESH,
        )

    def send(key, src, dst, dev):
        one = copy(key, src, dst, dev)
        one.start()
        started.append(one)

    def recv(key, land):
        if key not in arrived:
            arrived.add(key)
            copy(key, land, land, sib_dev).wait_recv()

    def loaded(*which):
        for k in which:
            if k not in present:
                present.add(k)
                loads[k].wait()

    def block(q, e, col, size):
        return cot_all.at[
            pl.ds(pl.multiple_of((q * n_expert + e) * ht, ht), ht), pl.ds(col, size)
        ]

    barrier = pltpu.get_barrier_semaphore()
    peers = [z_dev(i, core) for i in range(1, n_group) for core in (r, 1 - r)]
    peers += [x_dev, y_dev, d_dev, sib_dev]
    for dev in peers:
        pl.semaphore_signal(barrier, inc=1, device_id=dev, device_id_type=MESH)

    place = pltpu.make_async_copy(
        cot_hbm.at[pl.ds(pl.multiple_of(r * ht, ht), ht), :], block(g, ex, 0, width), lsem.at[0]
    )
    place.start()
    loads = [
        pltpu.make_async_copy(src, dst, lsem.at[1 + k])
        for k, (src, dst) in enumerate(
            [
                (sg_hbm.at[0], sg_all.at[r]),
                (su_hbm.at[0], su_all.at[r]),
                (wd_hbm.at[0], wd_ref),
                (wg_hbm.at[0], wg_ref),
                (wu_hbm.at[0], wu_ref),
            ]
        )
    ]
    for load in loads:
        load.start()

    named_by = lax.broadcasted_iota(jnp.int32, (experts, tok), 0)
    named = jnp.zeros((experts, tok), f32)
    weight = jnp.zeros((experts, tok), f32)
    for k in range(picks):
        same = ids_ref[k : k + 1, :] == named_by
        named = named + jnp.where(same, 1.0, 0.0)
        weight = weight + jnp.where(same, prob_ref[k : k + 1, :], 0.0)
    before = lax.broadcasted_iota(jnp.int32, (tok, tok), 0) < lax.broadcasted_iota(
        jnp.int32, (tok, tok), 1
    )
    slot = jnp.dot(
        named.astype(bf16), jnp.where(before, 1.0, 0.0).astype(bf16), preferred_element_type=f32
    )
    slot = jnp.where(named > 0.5, slot, -1.0)
    low_part = jnp.concatenate([slot[:, :ht], weight[:, :ht]], axis=1)
    high_part = jnp.concatenate([slot[:, ht:], weight[:, ht:]], axis=1)
    keep = jnp.where(r == 0, low_part, high_part)
    give = jnp.where(r == 0, high_part, low_part)
    blank = jnp.zeros((experts, tok), f32)

    def in_lanes(part):
        return jnp.concatenate(
            [jnp.where(r == 0, part, blank), jnp.where(r == 0, blank, part)], axis=1
        )

    keep, give = in_lanes(keep), in_lanes(give)
    for e in range(experts):
        meta_give[e] = give[e : e + 1, :]
    place.wait()
    pl.semaphore_wait(barrier, len(peers))

    def ag_cols(i, h):
        first = h * half + (raw_w if i == 1 else 0)
        size = ((half - raw_w) if i == 1 else half) // 2
        return (first, size), (first + size, size)

    def own(i, h):
        if i > 0:
            land_z(i, h)
        if i == 3:
            there = block(group_at(3), ex, h * half, half)
            send(("z", 2, h), there, there, z_dev(1))
        mine = wide_block(i, ex, h)
        send(("x", i, h), mine, mine, x_dev)
        send(("y", i, h), mine, mine, y_dev)

    def wide_block(i, e, h):
        (first, size), _ = ag_cols(i, h)
        return block(group_at(i), e, first, 2 * size)

    def land_z(i, h):
        recv(("z", i, h), block(group_at(i), ex, h * half, half))

    def land(name, i, h):
        if name in ("x", "y"):
            recv((name, i, h), wide_block(i, ex_x if name == "x" else ex_y, h))
        else:
            a, b = ag_cols(i, h)
            recv((name, i, h), block(group_at(i), ex_d, *(a if name == "fa" else b)))

    def fwa(i, h):
        land("x", i, h)
        there = block(group_at(i), ex_x, *ag_cols(i, h)[0])
        send(("fa", i, h), there, there, y_dev)

    def fwb(i, h):
        land("y", i, h)
        there = block(group_at(i), ex_y, *ag_cols(i, h)[1])
        send(("fb", i, h), there, there, x_dev)

    def raw(name, h):
        land({"x": "x", "y": "y", "d": "fa"}[name], 0, h)
        there = block(g, {"x": ex_x, "y": ex_y, "d": ex_d}[name], h * half, raw_w)
        send(("raw", name, h), there, there, z_dev(1))

    def chunk_here(i):
        for h in range(2):
            for name in ("x", "y", "fa", "fb"):
                land(name, i, h)
            if i > 0:
                land_z(i, h)
            if i == 1:
                for e, name in ((ex_x, "x"), (ex_y, "y"), (ex_d, "d")):
                    recv(("raw", name, h), block(group_at(1), e, h * half, raw_w))

    def z_out(i, h):
        mine = block(g, ex, h * half, half)
        send(("z", i, h), mine, mine, z_dev(i))

    def experts_of(plane):
        return pl.ds((plane // 2) * n_expert, n_expert)

    def metaz():
        recv(("give",), meta_take)
        for e in range(experts):
            meta_own[e] = keep[e : e + 1, :] + meta_take[e]
        for i in (3, 1, 2):
            send(("mz", i), meta_own.at[experts_of(group_at(i))], meta_z.at[i], z_dev(i))
        meta_z[0] = meta_own[experts_of(g)]

    def meta(i):
        if i > 0:
            recv(("mz", i), meta_z.at[i])
        for key, e, dev in (("mx", ex_x, x_dev), ("my", ex_y, y_dev), ("md", ex_d, d_dev)):
            send((key, i), meta_z.at[i, e], meta_all.at[i, ex], dev)

    def saved():
        send(("sg",), sg_hbm.at[0], sg_all.at[r], sib_dev)
        send(("su",), su_hbm.at[0], su_all.at[r], sib_dev)

    eye = lax.broadcasted_iota(jnp.int32, (2 * tok, 2 * tok), 0) == lax.broadcasted_iota(
        jnp.int32, (2 * tok, 2 * tok), 1
    )
    place_lane = lax.broadcasted_iota(jnp.int32, (ht, slots_g), 1).astype(f32)

    def rows_of(i):
        return pl.ds(pl.multiple_of(group_at(i) * rows_g, rows_g), rows_g)

    def factors(i):
        loaded(0, 1)
        recv(("sg",), sg_all.at[1 - r])
        recv(("su",), su_all.at[1 - r])
        for key, e in (("mx", ex_x), ("my", ex_y), ("md", ex_d)):
            recv((key, i), meta_all.at[i, e])
        meta_all[i, ex] = meta_z[i, ex]
        columns = []
        for b in range(n_expert):
            columns.append(jnp.sum(jnp.where(eye, meta_all[i, b], 0.0), axis=1, keepdims=True))
        slots = pl.ds(pl.multiple_of(group_at(i) * slots_g, slots_g), slots_g)
        to_gate = to_up = to_act = None
        for rho in range(2):
            picked, weights = [], []
            for b in range(n_expert):
                spot = columns[b][rho * tok : rho * tok + ht]
                spot = jnp.where(spot < -0.5, -1.0, spot + float(b * tok))
                picked.append(jnp.where(place_lane == spot, 1.0, 0.0))
                weights.append(columns[b][rho * tok + ht : (rho + 1) * tok])
            select = jnp.concatenate(picked, axis=0).astype(bf16)
            weights = jnp.concatenate(weights, axis=0)
            gate = jnp.dot(select, sg_all[rho, slots, :], preferred_element_type=f32)
            up = jnp.dot(select, su_all[rho, slots, :], preferred_element_type=f32)
            sig = jax.nn.sigmoid(gate)
            silu = gate * sig
            of_up = weights * silu
            of_act = of_up * up
            of_gate = weights * up * sig * (1.0 + gate * (1.0 - sig))
            to_gate = of_gate if rho == 0 else to_gate + of_gate
            to_up = of_up if rho == 0 else to_up + of_up
            to_act = of_act if rho == 0 else to_act + of_act
        f_gate[i] = to_gate
        f_up[i] = to_up
        act_all[rows_of(i), :] = to_act.astype(bf16)

    grads = []

    def hidden(i):
        chunk_here(i)
        loaded(2)
        d_act = lax.dot_general(
            cot_all[rows_of(i), :], wd_ref[...], NT, preferred_element_type=f32
        )
        grads[:] = [(d_act * f_gate[i]).astype(bf16), (d_act * f_up[i]).astype(bf16)]

    def partial(i, f):
        loaded(3, 4)
        first = (1 - r if f == 0 else r) * half
        wide = pl.ds(pl.multiple_of(first, half), half)
        value = lax.dot_general(grads[0], wg_ref[wide, :], NT, preferred_element_type=f32)
        value = value + lax.dot_general(
            grads[1], wu_ref[wide, :], NT, preferred_element_type=f32
        )
        value = value.reshape(2, 2, ht, half)
        if i == 0:
            own0[f] = value[:, :, :, :raw_w]
            p_buf[0, f, :, :, :, raw_w:] = value[:, :, :, raw_w:].astype(bf16)
            return
        p_buf[i, f] = value.astype(bf16)
        if i == 1:
            send(("merge", f), p_buf.at[1, f, :, :, :, pl.ds(0, raw_w)], rawr.at[f], z_dev(1))
        else:
            rs_first(i, f, "all")

    def merge(f):
        recv(("merge", f), rawr.at[f])
        value = own0[f] + rawr[f].astype(f32)
        p_buf[0, f, :, :, :, :raw_w] = value.astype(bf16)
        rs_first(0, f, "raw")

    def corner():
        send(("corner",), zs.at[0, 0], sibr, sib_dev)

    def rs_cols(i, part):
        first, size = (0, half)
        if part == "raw":
            first, size = 0, raw_w
        if part == "rest":
            first, size = raw_w, half - raw_w
        return pl.ds(first, size // 2), pl.ds(first + size // 2, size // 2), pl.ds(first, size)

    def rs_first(i, f, part):
        a, b, _ = rs_cols(i, part)
        send(("a1", i, f, part), p_buf.at[i, f, ny, :, :, a], r1.at[i, f, :, :, a], y_dev)
        send(("b1", i, f, part), p_buf.at[i, f, :, nx, :, b], r1.at[i, f, :, :, b], x_dev)

    def rs_second(i, f, part):
        a, b, _ = rs_cols(i, part)
        recv(("a1", i, f, part), r1.at[i, f, :, :, a])
        left = p_buf[i, f, y, :, :, a].astype(f32) + r1[i, f, :, :, a].astype(f32)
        s2[i, f, :, :, a] = left.astype(bf16)
        send(("a2", i, f, part), s2.at[i, f, nx, :, a], r2.at[i, f, :, a], x_dev)
        recv(("b1", i, f, part), r1.at[i, f, :, :, b])
        right = p_buf[i, f, :, x, :, b].astype(f32) + r1[i, f, :, :, b].astype(f32)
        s2[i, f, :, :, b] = right.astype(bf16)
        send(("b2", i, f, part), s2.at[i, f, ny, :, b], r2.at[i, f, :, b], y_dev)

    def rs_third(i, f, part):
        a, b, both = rs_cols(i, part)
        recv(("a2", i, f, part), r2.at[i, f, :, a])
        left = s2[i, f, x, :, a].astype(f32) + r2[i, f, :, a].astype(f32)
        zs[i, f, :, a] = left.astype(bf16)
        recv(("b2", i, f, part), r2.at[i, f, :, b])
        right = s2[i, f, y, :, b].astype(f32) + r2[i, f, :, b].astype(f32)
        zs[i, f, :, b] = right.astype(bf16)
        if i > 0:
            send(
                ("home", i, f),
                zs.at[i, f, :, both],
                zr.at[i, f, :, both],
                z_dev(i, 1 - r if f == 0 else r),
            )

    def grad_chunk(j):
        base = (1 - r if j < 2 else r) * half + (j % 2) * (half // 2)
        cols = pl.ds(pl.multiple_of(base, half // 2), half // 2)
        value = lax.dot_general(
            act_all[...], cot_all[:, cols], (((0,), (0,)), ((), ())), preferred_element_type=f32
        )
        part = pl.ds((j % 2) * (half // 2), half // 2)
        if j < 2:
            gt_send[:, part] = value.astype(bf16)
        else:
            recv(("grad",), gt_recv)
            gd_ref[:, part] = value + gt_recv[:, part].astype(f32)
        if j == 1:
            send(("grad",), gt_send, gt_recv, sib_dev)

    def drain():
        while started:
            started.pop(0).wait_send()

    steps = {
        "zo": z_out,
        "own": own,
        "fwa": fwa,
        "fwb": fwb,
        "raw": raw,
        "metaz": metaz,
        "meta": meta,
        "saved": saved,
        "fac": factors,
        "hid": hidden,
        "par": partial,
        "rs1": rs_first,
        "mrg": merge,
        "rs2": rs_second,
        "rs3": rs_third,
        "corner": corner,
        "drain": drain,
        "grad": grad_chunk,
    }
    send(("give",), meta_give, meta_take, sib_dev)
    for name, *where in SCHEDULE:
        steps[name](*where)

    front, back = pl.ds(0, raw_w), pl.ds(raw_w, half - raw_w)

    def finish(own, f, rows):
        for i, cols in ((3, pl.ds(0, half)), (1, back), (2, pl.ds(0, half))):
            recv(("home", i, f), zr.at[i, f, :, cols])
        if f == 0:
            recv(("corner",), sibr)
        for cols in (front, back):
            total = own[:, cols].astype(f32)
            for i in (3, 2) if cols is front else (3, 1, 2):
                total = total + zr[i, f, :, cols].astype(f32)
            out_ref[rows, cols] = total.astype(bf16)

    finish(zs.at[0, 1], 1, pl.ds(pl.multiple_of(r * ht, ht), ht))
    finish(sibr, 0, pl.ds(pl.multiple_of((1 - r) * ht, ht), ht))
    drain()


def finish_kernel(rows_ref, down_ref, out_hbm, gd_hbm, sems):
    rows = down_ref.shape[0] // 2
    copies = [pltpu.make_async_copy(rows_ref, out_hbm, sems.at[2])]
    for k in range(2):
        part = pl.ds(k * rows, rows)
        copies.append(
            pltpu.make_async_copy(down_ref.at[part, :], gd_hbm.at[0, part, :], sems.at[k])
        )
    for copy in copies:
        copy.start()
    for copy in copies:
        copy.wait()


def dense_plan(cotangent, expert_ids, gate_probs, saved_gate, saved_up, w_gate, w_up, w_down):
    n_group = lax.axis_size("group")
    n_expert = lax.axis_size("expert")
    tok, width = cotangent.shape
    half, quarter = width // 2, width // 4
    hidden = w_down.shape[1]
    experts = n_group * n_expert // 2
    blocks = n_group * n_expert
    rows_g = n_expert * tok // 2
    bf16, f32 = jnp.bfloat16, jnp.float32
    vmem = pl.BlockSpec(memory_space=pltpu.VMEM)
    ht = tok // 2
    raw_w = quarter
    copies = 128
    cotangent, saved_gate, saved_up, w_gate, w_up, w_down = (
        pltpu.with_memory_space_constraint(value, pltpu.HBM)
        for value in (cotangent, saved_gate, saved_up, w_gate, w_up, w_down)
    )
    ids, probs = (
        pltpu.with_memory_space_constraint(value[0].T, pltpu.HBM)
        for value in (expert_ids, gate_probs)
    )
    here = pl.BlockSpec(memory_space=pltpu.HBM)
    rows, down = pl.pallas_call(
        functools.partial(dense_kernel, n_group, n_expert),
        out_shape=(
            jax.ShapeDtypeStruct((tok, half), bf16),
            jax.ShapeDtypeStruct((hidden, half), f32),
        ),
        in_specs=[here, vmem, vmem] + [here] * 5,
        out_specs=(vmem, vmem),
        scratch_shapes=[
            pltpu.VMEM((2,) + saved_gate.shape[1:], bf16),
            pltpu.VMEM((2,) + saved_up.shape[1:], bf16),
            pltpu.VMEM(w_gate.shape[1:], bf16),
            pltpu.VMEM(w_up.shape[1:], bf16),
            pltpu.VMEM(w_down.shape[1:], bf16),
            pltpu.VMEM((blocks * ht, width), bf16),
            pltpu.VMEM((experts, 1, 2 * tok), f32),
            pltpu.VMEM((experts, 1, 2 * tok), f32),
            pltpu.VMEM((experts, 1, 2 * tok), f32),
            pltpu.VMEM((n_group, n_expert, 1, 2 * tok), f32),
            pltpu.VMEM((n_group, n_expert, 1, 2 * tok), f32),
            pltpu.VMEM((blocks * ht, hidden), bf16),
            pltpu.VMEM((n_group, rows_g, hidden), f32),
            pltpu.VMEM((n_group, rows_g, hidden), f32),
            pltpu.VMEM((n_group, 2, 2, 2, ht, half), bf16),
            pltpu.VMEM((2, 2, 2, ht, raw_w), f32),
            pltpu.VMEM((2, 2, 2, ht, raw_w), bf16),
            pltpu.VMEM((n_group, 2, 2, ht, half), bf16),
            pltpu.VMEM((n_group, 2, 2, ht, half), bf16),
            pltpu.VMEM((n_group, 2, ht, half), bf16),
            pltpu.VMEM((n_group, 2, ht, half), bf16),
            pltpu.VMEM((n_group, 2, ht, half), bf16),
            pltpu.VMEM((ht, half), bf16),
            pltpu.VMEM((hidden, half), bf16),
            pltpu.VMEM((hidden, half), bf16),
            pltpu.SemaphoreType.DMA((copies,)),
            pltpu.SemaphoreType.DMA((copies,)),
            pltpu.SemaphoreType.DMA((6,)),
        ],
        compiler_params=pltpu.CompilerParams(
            collective_id=0, has_side_effects=True, vmem_limit_bytes=40 * 1024 * 1024
        ),
    )(
        cotangent,
        ids,
        probs,
        saved_gate,
        saved_up,
        w_gate,
        w_up,
        w_down,
    )
    return pl.pallas_call(
        finish_kernel,
        out_shape=(
            jax.ShapeDtypeStruct((tok, half), bf16),
            jax.ShapeDtypeStruct((1, hidden, half), f32),
        ),
        in_specs=[vmem] * 2,
        out_specs=(here, here),
        scratch_shapes=[pltpu.SemaphoreType.DMA((3,))],
        compiler_params=pltpu.CompilerParams(vmem_limit_bytes=8 * 1024 * 1024),
    )(rows, down)


def on_device(cotangent, expert_ids, gate_probs, saved_gate, saved_up, w_gate, w_up, w_down):
    n_group = lax.axis_size("group")
    n_expert = lax.axis_size("expert")
    n_replica = lax.axis_size("replica")
    tok_rows = cotangent.shape[0]
    capacity = saved_gate.shape[1] // (n_group * n_expert)
    small = n_group == 4 and n_expert == 4 and n_replica == 2
    plan = routed_plan
    if small and capacity == tok_rows and 2 * tok_rows == 128:
        plan = dense_plan
    return plan(cotangent, expert_ids, gate_probs, saved_gate, saved_up, w_gate, w_up, w_down)


def solution(mesh):
    return jax.shard_map(
        on_device,
        mesh=mesh,
        in_specs=(
            P(("group", "expert"), None),
            P("replica", ("group", "expert"), None),
            P("replica", ("group", "expert"), None),
            P(("group", "expert"), "replica", None),
            P(("group", "expert"), "replica", None),
            P(("group", "expert"), None, None),
            P(("group", "expert"), None, None),
            P(("group", "expert"), None, None),
        ),
        out_specs=(P(("group", "expert"), "replica"), P(("group", "expert"), None, "replica")),
        check_vma=False,
    )
```

```python
import functools

import jax
import jax.numpy as jnp
from jax import lax
from jax.experimental import pallas as pl
from jax.experimental.pallas import tpu as pltpu
from jax.sharding import PartitionSpec as P

MESH = pl.DeviceIdType.MESH
NT = (((1,), (1,)), ((), ()))


def from_partner(value, axis, bit):
    mask = 2**bit
    pairs = [(source, source ^ mask) for source in range(lax.axis_size(axis))]
    return lax.ppermute(value, axis, pairs)


def routed_plan(cotangent, expert_ids, gate_probs, saved_gate, saved_up, w_gate, w_up, w_down):
    n_group = lax.axis_size("group")
    n_expert = lax.axis_size("expert")
    tok_rows, model_width = cotangent.shape
    pick_count = expert_ids.shape[2]
    experts = n_group * n_expert // 2
    half_width = model_width // 2
    capacity = saved_gate.shape[1] // (n_group * n_expert)
    assigned = tok_rows * pick_count
    flat_ids = expert_ids.reshape(assigned)
    positions = jnp.arange(assigned, dtype=jnp.int32)
    same_expert = (flat_ids[:, None] == flat_ids[None, :]) & (
        positions[None, :] < positions[:, None]
    )
    slot_pos = jnp.sum(same_expert.astype(jnp.int32), axis=1)
    target = flat_ids * capacity + slot_pos
    places = jnp.arange(experts * capacity, dtype=jnp.int32)
    dispatch_map = (places[:, None] == target[None, :]).astype(jnp.bfloat16)
    scaled = (gate_probs[0][:, :, None] * cotangent[:, None, :].astype(jnp.float32)).astype(
        jnp.bfloat16
    )
    scaled = scaled.reshape(assigned, model_width)
    packed = jnp.dot(dispatch_map, scaled, preferred_element_type=jnp.float32).astype(jnp.bfloat16)
    packed = packed.reshape(n_group // 2, n_expert, capacity, 2, half_width)
    packed = packed.transpose(0, 3, 1, 2, 4).reshape(n_group, n_expert, capacity, half_width)
    arrived = lax.all_to_all(
        lax.all_to_all(packed, "expert", split_axis=1, concat_axis=1, tiled=True),
        "group",
        split_axis=0,
        concat_axis=0,
        tiled=True,
    )
    partner = from_partner(arrived, "group", 0)
    low_half = lax.axis_index("group") % 2 == 0
    front_half = jnp.where(low_half, arrived, partner)
    back_half = jnp.where(low_half, partner, arrived)
    dy_slots = jnp.concatenate([front_half, back_half], axis=3).reshape(-1, model_width)
    pre_gate = saved_gate[0].astype(jnp.float32)
    pre_up = saved_up[0].astype(jnp.float32)
    sigmoid_gate = jax.nn.sigmoid(pre_gate)
    silu_gate = pre_gate * sigmoid_gate
    activation = (silu_gate * pre_up).astype(jnp.bfloat16)
    d_act = lax.dot_general(
        dy_slots, w_down[0], (((1,), (1,)), ((), ())), preferred_element_type=jnp.float32
    )
    d_gate = (d_act * pre_up * sigmoid_gate * (1.0 + pre_gate * (1.0 - sigmoid_gate))).astype(
        jnp.bfloat16
    )
    d_up = (d_act * silu_gate).astype(jnp.bfloat16)
    partial_value = lax.dot_general(
        d_gate, w_gate[0], (((1,), (1,)), ((), ())), preferred_element_type=jnp.float32
    )
    partial_value = partial_value + lax.dot_general(
        d_up, w_up[0], (((1,), (1,)), ((), ())), preferred_element_type=jnp.float32
    )
    partial_value = partial_value.astype(jnp.bfloat16)
    own_half = jnp.where(low_half, partial_value[:, :half_width], partial_value[:, half_width:])
    peer_half = jnp.where(low_half, partial_value[:, half_width:], partial_value[:, :half_width])
    received = from_partner(peer_half, "group", 0)
    combined = (own_half.astype(jnp.float32) + received.astype(jnp.float32)).astype(jnp.bfloat16)
    combined = combined.reshape(n_group, n_expert, capacity, half_width)
    grad_terms = lax.dot_general(
        activation, dy_slots, (((0,), (0,)), ((), ())), preferred_element_type=jnp.float32
    )
    returned = lax.all_to_all(
        lax.all_to_all(combined, "group", split_axis=0, concat_axis=0, tiled=True),
        "expert",
        split_axis=1,
        concat_axis=1,
        tiled=True,
    )
    home_rows = returned.reshape(n_group // 2, 2, n_expert, capacity, half_width)
    home_rows = home_rows.transpose(0, 2, 3, 1, 4).reshape(experts * capacity, model_width)
    per_assign = lax.dot_general(
        dispatch_map, home_rows, (((0,), (0,)), ((), ())), preferred_element_type=jnp.float32
    )
    home_sum = jnp.sum(per_assign.reshape(tok_rows, pick_count, model_width), axis=1)
    grad_down, grad_input = (
        lax.psum_scatter(grad_terms, "replica", scatter_dimension=1, tiled=True),
        lax.psum_scatter(home_sum, "replica", scatter_dimension=1, tiled=True),
    )
    return (grad_input.astype(jnp.bfloat16), grad_down[None])


SCHEDULE = (
    ("zo", 3, 0), ("own", 0, 0), ("saved",), ("zo", 1, 1), ("own", 0, 1), ("metaz",),
    ("meta", 0), ("zo", 3, 1), ("fwa", 0, 0), ("fwb", 0, 0), ("own", 3, 0), ("raw", "x"),
    ("fwa", 0, 1), ("fwb", 0, 1), ("fac", 0), ("own", 1, 1), ("own", 3, 1), ("own", 2, 0),
    ("fwa", 3, 0), ("meta", 1), ("meta", 3), ("zo", 1, 0), ("hid", 0), ("raw", "d"),
    ("meta", 2), ("fwb", 3, 0), ("fwb", 3, 1), ("fwa", 3, 1), ("par", 0, 1), ("own", 2, 1),
    ("raw", "y"), ("par", 0, 0), ("fwa", 1, 1), ("fwb", 2, 0), ("fwb", 1, 1), ("fwa", 2, 0),
    ("fac", 1), ("fac", 3), ("hid", 3), ("par", 3, 1), ("fwb", 2, 1), ("fwa", 2, 1),
    ("par", 3, 0), ("hid", 1), ("par", 1, 0), ("par", 1, 1), ("fac", 2), ("rs2", 3, 1),
    ("hid", 2), ("par", 2, 1), ("rs2", 3, 0), ("par", 2, 0), ("rs1", 0, 1), ("rs3", 3, 1),
    ("rs2", 2, 1), ("grad", 0), ("rs2", 1, 1), ("rs3", 3, 0), ("mrg", 0), ("grad", 1),
    ("mrg", 1), ("rs2", 2, 0), ("grad", 2), ("grad", 3), ("rs2", 0, 1), ("rs3", 2, 1),
    ("rs3", 1, 1), ("rs2", 0, 0), ("rs3", 2, 0), ("rs3", 0, 1), ("drain",), ("rs3", 0, 0),
    ("corner",),
)


def dense_kernel(
    n_group,
    n_expert,
    cot_hbm,
    ids_hbm,
    prob_hbm,
    sg_hbm,
    su_hbm,
    wg_hbm,
    wu_hbm,
    wd_hbm,
    out_ref,
    gd_ref,
    ids_ref,
    prob_ref,
    sg_all,
    su_all,
    wg_ref,
    wu_ref,
    wd_ref,
    cot_all,
    meta_own,
    meta_give,
    meta_take,
    meta_z,
    meta_all,
    act_all,
    f_gate,
    f_up,
    p_buf,
    own0,
    rawr,
    r1,
    s2,
    r2,
    zs,
    zr,
    sibr,
    gt_send,
    gt_recv,
    ssem,
    rsem,
    lsem,
):
    tok, width = cot_hbm.shape
    ht = tok // 2
    half = width // 2
    front, back = pl.ds(0, half // 2), pl.ds(half // 2, half // 2)
    rows_g = n_expert * ht
    slots_g = n_expert * tok
    picks = ids_ref.shape[0]
    experts = meta_own.shape[0]
    f32, bf16 = jnp.float32, jnp.bfloat16
    g = lax.axis_index("group")
    ex = lax.axis_index("expert")
    r = lax.axis_index("replica")
    x, y = ex % 2, ex // 2
    nx, ny = 1 - x, 1 - y
    ex_x, ex_y, ex_d = y * 2 + nx, ny * 2 + x, ny * 2 + nx
    x_dev, y_dev, d_dev = (g, ex_x, r), (g, ex_y, r), (g, ex_d, r)
    sib_dev = (g, ex, 1 - r)

    def group_at(i):
        low = (g % 2 + i % 2) % 2
        high = (g // 2 + i // 2) % 2
        return low + 2 * high

    def z_dev(i, core=None):
        return (group_at(i), ex, r if core is None else core)

    number = {}
    started, arrived, present = [], set(), set()

    def copy(key, src, dst, dev):
        k = number.setdefault(key, len(number))
        return pltpu.make_async_remote_copy(
            src_ref=src,
            dst_ref=dst,
            send_sem=ssem.at[k],
            recv_sem=rsem.at[k],
            device_id=dev,
            device_id_type=MESH,
        )

    def send(key, src, dst, dev):
        one = copy(key, src, dst, dev)
        one.start()
        started.append(one)

    def recv(key, land):
        if key not in arrived:
            arrived.add(key)
            copy(key, land, land, sib_dev).wait_recv()

    def loaded(*which):
        for k in which:
            if k not in present:
                present.add(k)
                loads[k].wait()

    def block(q, e, col, size):
        return cot_all.at[
            pl.ds(pl.multiple_of((q * n_expert + e) * ht, ht), ht), pl.ds(col, size)
        ]

    barrier = pltpu.get_barrier_semaphore()
    peers = [z_dev(i, core) for i in range(1, n_group) for core in (r, 1 - r)]
    peers += [x_dev, y_dev, d_dev, sib_dev]
    for dev in peers:
        pl.semaphore_signal(barrier, inc=1, device_id=dev, device_id_type=MESH)

    routing = [
        pltpu.make_async_copy(ids_hbm, ids_ref, lsem.at[6]),
        pltpu.make_async_copy(prob_hbm, prob_ref, lsem.at[7]),
    ]
    for load in routing:
        load.start()
    place = pltpu.make_async_copy(
        cot_hbm.at[pl.ds(pl.multiple_of(r * ht, ht), ht), :], block(g, ex, 0, width), lsem.at[0]
    )
    place.start()
    loads = [
        pltpu.make_async_copy(src, dst, lsem.at[1 + k])
        for k, (src, dst) in enumerate(
            [
                (sg_hbm.at[0], sg_all.at[r]),
                (su_hbm.at[0], su_all.at[r]),
                (wd_hbm.at[0], wd_ref),
                (wg_hbm.at[0], wg_ref),
                (wu_hbm.at[0], wu_ref),
            ]
        )
    ]
    for load in loads:
        load.start()

    for load in routing:
        load.wait()
    named_by = lax.broadcasted_iota(jnp.int32, (experts, tok), 0)
    named = jnp.zeros((experts, tok), f32)
    weight = jnp.zeros((experts, tok), f32)
    for k in range(picks):
        same = ids_ref[k : k + 1, :] == named_by
        named = named + jnp.where(same, 1.0, 0.0)
        weight = weight + jnp.where(same, prob_ref[k : k + 1, :], 0.0)
    before = lax.broadcasted_iota(jnp.int32, (tok, tok), 0) < lax.broadcasted_iota(
        jnp.int32, (tok, tok), 1
    )
    slot = jnp.dot(
        named.astype(bf16), jnp.where(before, 1.0, 0.0).astype(bf16), preferred_element_type=f32
    )
    slot = jnp.where(named > 0.5, slot, -1.0)
    low_part = jnp.concatenate([slot[:, :ht], weight[:, :ht]], axis=1)
    high_part = jnp.concatenate([slot[:, ht:], weight[:, ht:]], axis=1)
    keep = jnp.where(r == 0, low_part, high_part)
    give = jnp.where(r == 0, high_part, low_part)
    blank = jnp.zeros((experts, tok), f32)

    def in_lanes(part):
        return jnp.concatenate(
            [jnp.where(r == 0, part, blank), jnp.where(r == 0, blank, part)], axis=1
        )

    keep, give = in_lanes(keep), in_lanes(give)
    for e in range(experts):
        meta_give[e] = give[e : e + 1, :]
    place.wait()
    pl.semaphore_wait(barrier, len(peers))

    def ag_cols(h):
        first, size = h * half, half // 2
        return (first, size), (first + size, size)

    def own(i, h):
        if i > 0:
            land_z(i, h)
        if i == 3:
            there = block(group_at(3), ex, h * half, half)
            send(("z", 2, h), there, there, z_dev(1))
        mine = wide_block(i, ex, h)
        send(("x", i, h), mine, mine, x_dev)
        send(("y", i, h), mine, mine, y_dev)

    def wide_block(i, e, h):
        return block(group_at(i), e, h * half, half)

    def land_z(i, h):
        recv(("z", i, h), block(group_at(i), ex, h * half, half))

    def land(name, i, h):
        if name in ("x", "y"):
            recv((name, i, h), wide_block(i, ex_x if name == "x" else ex_y, h))
        else:
            a, b = ag_cols(h)
            recv((name, i, h), block(group_at(i), ex_d, *(a if name == "fa" else b)))

    def fwa(i, h):
        land("x", i, h)
        there = block(group_at(i), ex_x, *ag_cols(h)[0])
        send(("fa", i, h), there, there, y_dev)

    def fwb(i, h):
        land("y", i, h)
        there = block(group_at(i), ex_y, *ag_cols(h)[1])
        send(("fb", i, h), there, there, x_dev)

    def raw(name):
        for part in ("fa", "fb") if name == "d" else (name,):
            land(part, 0, 0)
        there = wide_block(0, {"x": ex_x, "y": ex_y, "d": ex_d}[name], 0)
        send(("raw", name), there, there, z_dev(1))

    def chunk_here(i):
        for h in range(2):
            if i > 0:
                land_z(i, h)
            if (i, h) == (1, 0):
                for e, name in ((ex_x, "x"), (ex_y, "y"), (ex_d, "d")):
                    recv(("raw", name), wide_block(1, e, 0))
                continue
            for name in ("x", "y", "fa", "fb"):
                land(name, i, h)

    def z_out(i, h):
        mine = block(g, ex, h * half, half)
        send(("z", i, h), mine, mine, z_dev(i))

    def experts_of(plane):
        return pl.ds((plane // 2) * n_expert, n_expert)

    def metaz():
        recv(("give",), meta_take)
        for e in range(experts):
            meta_own[e] = keep[e : e + 1, :] + meta_take[e]
        for i in (3, 1, 2):
            send(("mz", i), meta_own.at[experts_of(group_at(i))], meta_z.at[i], z_dev(i))
        meta_z[0] = meta_own[experts_of(g)]

    def meta(i):
        if i > 0:
            recv(("mz", i), meta_z.at[i])
        for key, e, dev in (("mx", ex_x, x_dev), ("my", ex_y, y_dev), ("md", ex_d, d_dev)):
            send((key, i), meta_z.at[i, e], meta_all.at[i, ex], dev)

    def saved():
        send(("sg",), sg_hbm.at[0], sg_all.at[r], sib_dev)
        send(("su",), su_hbm.at[0], su_all.at[r], sib_dev)

    eye = lax.broadcasted_iota(jnp.int32, (2 * tok, 2 * tok), 0) == lax.broadcasted_iota(
        jnp.int32, (2 * tok, 2 * tok), 1
    )
    place_lane = lax.broadcasted_iota(jnp.int32, (ht, slots_g), 1).astype(f32)

    def rows_of(i):
        return pl.ds(pl.multiple_of(group_at(i) * rows_g, rows_g), rows_g)

    def factors(i):
        loaded(0, 1)
        recv(("sg",), sg_all.at[1 - r])
        recv(("su",), su_all.at[1 - r])
        for key, e in (("mx", ex_x), ("my", ex_y), ("md", ex_d)):
            recv((key, i), meta_all.at[i, e])
        meta_all[i, ex] = meta_z[i, ex]
        columns = []
        for b in range(n_expert):
            columns.append(jnp.sum(jnp.where(eye, meta_all[i, b], 0.0), axis=1, keepdims=True))
        slots = pl.ds(pl.multiple_of(group_at(i) * slots_g, slots_g), slots_g)
        to_gate = to_up = to_act = None
        for rho in range(2):
            picked, weights = [], []
            for b in range(n_expert):
                spot = columns[b][rho * tok : rho * tok + ht]
                spot = jnp.where(spot < -0.5, -1.0, spot + float(b * tok))
                picked.append(jnp.where(place_lane == spot, 1.0, 0.0))
                weights.append(columns[b][rho * tok + ht : (rho + 1) * tok])
            select = jnp.concatenate(picked, axis=0).astype(bf16)
            weights = jnp.concatenate(weights, axis=0)
            gate = jnp.dot(select, sg_all[rho, slots, :], preferred_element_type=f32)
            up = jnp.dot(select, su_all[rho, slots, :], preferred_element_type=f32)
            sig = jax.nn.sigmoid(gate)
            silu = gate * sig
            of_up = weights * silu
            of_act = of_up * up
            of_gate = weights * up * sig * (1.0 + gate * (1.0 - sig))
            to_gate = of_gate if rho == 0 else to_gate + of_gate
            to_up = of_up if rho == 0 else to_up + of_up
            to_act = of_act if rho == 0 else to_act + of_act
        f_gate[i] = to_gate
        f_up[i] = to_up
        act_all[rows_of(i), :] = to_act.astype(bf16)

    grads = []

    def hidden(i):
        chunk_here(i)
        loaded(2)
        d_act = lax.dot_general(
            cot_all[rows_of(i), :], wd_ref[...], NT, preferred_element_type=f32
        )
        grads[:] = [(d_act * f_gate[i]).astype(bf16), (d_act * f_up[i]).astype(bf16)]

    def partial(i, f):
        loaded(3, 4)
        first = (1 - r if f == 0 else r) * half
        wide = pl.ds(pl.multiple_of(first, half), half)
        value = lax.dot_general(grads[0], wg_ref[wide, :], NT, preferred_element_type=f32)
        value = value + lax.dot_general(
            grads[1], wu_ref[wide, :], NT, preferred_element_type=f32
        )
        value = value.reshape(2, 2, ht, half)
        if (i, f) == (0, 0):
            own0[...] = value
            return
        p_buf[i, f] = value.astype(bf16)
        if (i, f) == (1, 0):
            for part in (front, back):
                send(
                    ("merge", part is back),
                    p_buf.at[1, 0, :, :, :, part],
                    rawr.at[:, :, :, part],
                    z_dev(1),
                )
        elif i > 0:
            rs_first(i, f)

    def merge(c):
        part = back if c else front
        recv(("merge", bool(c)), rawr.at[:, :, :, part])
        value = own0[:, :, :, part] + rawr[:, :, :, part].astype(f32)
        p_buf[0, 0, :, :, :, part] = value.astype(bf16)
        if c:
            rs_first_b(0, 0)
        else:
            rs_first_a(0, 0)

    def corner():
        send(("corner",), zs.at[0, 0], sibr, sib_dev)

    def rs_first_a(i, f):
        send(("a1", i, f), p_buf.at[i, f, ny, :, :, front], r1.at[i, f, :, :, front], y_dev)

    def rs_first_b(i, f):
        send(("b1", i, f), p_buf.at[i, f, :, nx, :, back], r1.at[i, f, :, :, back], x_dev)

    def rs_first(i, f):
        rs_first_a(i, f)
        rs_first_b(i, f)

    def rs_second(i, f):
        recv(("a1", i, f), r1.at[i, f, :, :, front])
        left = p_buf[i, f, y, :, :, front].astype(f32) + r1[i, f, :, :, front].astype(f32)
        s2[i, f, :, :, front] = left.astype(bf16)
        send(("a2", i, f), s2.at[i, f, nx, :, front], r2.at[i, f, :, front], x_dev)
        recv(("b1", i, f), r1.at[i, f, :, :, back])
        right = p_buf[i, f, :, x, :, back].astype(f32) + r1[i, f, :, :, back].astype(f32)
        s2[i, f, :, :, back] = right.astype(bf16)
        send(("b2", i, f), s2.at[i, f, ny, :, back], r2.at[i, f, :, back], y_dev)

    def rs_third(i, f):
        recv(("a2", i, f), r2.at[i, f, :, front])
        left = s2[i, f, x, :, front].astype(f32) + r2[i, f, :, front].astype(f32)
        zs[i, f, :, front] = left.astype(bf16)
        recv(("b2", i, f), r2.at[i, f, :, back])
        right = s2[i, f, y, :, back].astype(f32) + r2[i, f, :, back].astype(f32)
        zs[i, f, :, back] = right.astype(bf16)
        if i > 0:
            send(("home", i, f), zs.at[i, f], zr.at[i, f], z_dev(i, 1 - r if f == 0 else r))

    def grad_chunk(j):
        base = (1 - r if j < 2 else r) * half + (j % 2) * (half // 2)
        cols = pl.ds(pl.multiple_of(base, half // 2), half // 2)
        value = lax.dot_general(
            act_all[...], cot_all[:, cols], (((0,), (0,)), ((), ())), preferred_element_type=f32
        )
        part = pl.ds((j % 2) * (half // 2), half // 2)
        if j < 2:
            gt_send[:, part] = value.astype(bf16)
        else:
            recv(("grad",), gt_recv)
            gd_ref[:, part] = value + gt_recv[:, part].astype(f32)
        if j == 1:
            send(("grad",), gt_send, gt_recv, sib_dev)

    def drain():
        while started:
            started.pop(0).wait_send()

    steps = {
        "zo": z_out,
        "own": own,
        "fwa": fwa,
        "fwb": fwb,
        "raw": raw,
        "metaz": metaz,
        "meta": meta,
        "saved": saved,
        "fac": factors,
        "hid": hidden,
        "par": partial,
        "rs1": rs_first,
        "mrg": merge,
        "rs2": rs_second,
        "rs3": rs_third,
        "corner": corner,
        "drain": drain,
        "grad": grad_chunk,
    }
    send(("give",), meta_give, meta_take, sib_dev)
    for name, *where in SCHEDULE:
        steps[name](*where)

    def finish(own, f, rows):
        near = (3, 2) if f == 0 else (3, 1, 2)
        for i in near:
            recv(("home", i, f), zr.at[i, f])
        if f == 0:
            recv(("corner",), sibr)
        total = own[...].astype(f32)
        for i in near:
            total = total + zr[i, f].astype(f32)
        out_ref[rows, :] = total.astype(bf16)

    finish(zs.at[0, 1], 1, pl.ds(pl.multiple_of(r * ht, ht), ht))
    finish(sibr, 0, pl.ds(pl.multiple_of((1 - r) * ht, ht), ht))
    drain()


def finish_kernel(rows_ref, down_ref, out_hbm, gd_hbm, sems):
    rows = down_ref.shape[0] // 2
    copies = [pltpu.make_async_copy(rows_ref, out_hbm, sems.at[2])]
    for k in range(2):
        part = pl.ds(k * rows, rows)
        copies.append(
            pltpu.make_async_copy(down_ref.at[part, :], gd_hbm.at[0, part, :], sems.at[k])
        )
    for copy in copies:
        copy.start()
    for copy in copies:
        copy.wait()


def dense_plan(cotangent, expert_ids, gate_probs, saved_gate, saved_up, w_gate, w_up, w_down):
    n_group = lax.axis_size("group")
    n_expert = lax.axis_size("expert")
    tok, width = cotangent.shape
    half = width // 2
    hidden = w_down.shape[1]
    experts = n_group * n_expert // 2
    blocks = n_group * n_expert
    rows_g = n_expert * tok // 2
    bf16, f32 = jnp.bfloat16, jnp.float32
    vmem = pl.BlockSpec(memory_space=pltpu.VMEM)
    ht = tok // 2
    copies = 96
    cotangent, saved_gate, saved_up, w_gate, w_up, w_down = (
        pltpu.with_memory_space_constraint(value, pltpu.HBM)
        for value in (cotangent, saved_gate, saved_up, w_gate, w_up, w_down)
    )
    ids, probs = (
        pltpu.with_memory_space_constraint(value[0].T, pltpu.HBM)
        for value in (expert_ids, gate_probs)
    )
    here = pl.BlockSpec(memory_space=pltpu.HBM)
    rows, down = pl.pallas_call(
        functools.partial(dense_kernel, n_group, n_expert),
        out_shape=(
            jax.ShapeDtypeStruct((tok, half), bf16),
            jax.ShapeDtypeStruct((hidden, half), f32),
        ),
        in_specs=[here] * 8,
        out_specs=(vmem, vmem),
        scratch_shapes=[
            pltpu.VMEM(ids.shape, jnp.int32),
            pltpu.VMEM(probs.shape, f32),
            pltpu.VMEM((2,) + saved_gate.shape[1:], bf16),
            pltpu.VMEM((2,) + saved_up.shape[1:], bf16),
            pltpu.VMEM(w_gate.shape[1:], bf16),
            pltpu.VMEM(w_up.shape[1:], bf16),
            pltpu.VMEM(w_down.shape[1:], bf16),
            pltpu.VMEM((blocks * ht, width), bf16),
            pltpu.VMEM((experts, 1, 2 * tok), f32),
            pltpu.VMEM((experts, 1, 2 * tok), f32),
            pltpu.VMEM((experts, 1, 2 * tok), f32),
            pltpu.VMEM((n_group, n_expert, 1, 2 * tok), f32),
            pltpu.VMEM((n_group, n_expert, 1, 2 * tok), f32),
            pltpu.VMEM((blocks * ht, hidden), bf16),
            pltpu.VMEM((n_group, rows_g, hidden), f32),
            pltpu.VMEM((n_group, rows_g, hidden), f32),
            pltpu.VMEM((n_group, 2, 2, 2, ht, half), bf16),
            pltpu.VMEM((2, 2, ht, half), f32),
            pltpu.VMEM((2, 2, ht, half), bf16),
            pltpu.VMEM((n_group, 2, 2, ht, half), bf16),
            pltpu.VMEM((n_group, 2, 2, ht, half), bf16),
            pltpu.VMEM((n_group, 2, ht, half), bf16),
            pltpu.VMEM((n_group, 2, ht, half), bf16),
            pltpu.VMEM((n_group, 2, ht, half), bf16),
            pltpu.VMEM((ht, half), bf16),
            pltpu.VMEM((hidden, half), bf16),
            pltpu.VMEM((hidden, half), bf16),
            pltpu.SemaphoreType.DMA((copies,)),
            pltpu.SemaphoreType.DMA((copies,)),
            pltpu.SemaphoreType.DMA((8,)),
        ],
        compiler_params=pltpu.CompilerParams(
            collective_id=0, has_side_effects=True, vmem_limit_bytes=40 * 1024 * 1024
        ),
    )(
        cotangent,
        ids,
        probs,
        saved_gate,
        saved_up,
        w_gate,
        w_up,
        w_down,
    )
    return pl.pallas_call(
        finish_kernel,
        out_shape=(
            jax.ShapeDtypeStruct((tok, half), bf16),
            jax.ShapeDtypeStruct((1, hidden, half), f32),
        ),
        in_specs=[vmem] * 2,
        out_specs=(here, here),
        scratch_shapes=[pltpu.SemaphoreType.DMA((3,))],
        compiler_params=pltpu.CompilerParams(vmem_limit_bytes=8 * 1024 * 1024),
    )(rows, down)


def on_device(cotangent, expert_ids, gate_probs, saved_gate, saved_up, w_gate, w_up, w_down):
    n_group = lax.axis_size("group")
    n_expert = lax.axis_size("expert")
    n_replica = lax.axis_size("replica")
    tok_rows = cotangent.shape[0]
    capacity = saved_gate.shape[1] // (n_group * n_expert)
    small = n_group == 4 and n_expert == 4 and n_replica == 2
    plan = routed_plan
    if small and capacity == tok_rows and 2 * tok_rows == 128:
        plan = dense_plan
    return plan(cotangent, expert_ids, gate_probs, saved_gate, saved_up, w_gate, w_up, w_down)


def solution(mesh):
    return jax.shard_map(
        on_device,
        mesh=mesh,
        in_specs=(
            P(("group", "expert"), None),
            P("replica", ("group", "expert"), None),
            P("replica", ("group", "expert"), None),
            P(("group", "expert"), "replica", None),
            P(("group", "expert"), "replica", None),
            P(("group", "expert"), None, None),
            P(("group", "expert"), None, None),
            P(("group", "expert"), None, None),
        ),
        out_specs=(P(("group", "expert"), "replica"), P(("group", "expert"), None, "replica")),
        check_vma=False,
    )
```

```python
import functools

import jax
import jax.numpy as jnp
from jax import lax
from jax.experimental import pallas as pl
from jax.experimental.pallas import tpu as pltpu
from jax.sharding import PartitionSpec as P

MESH = pl.DeviceIdType.MESH
NT = (((1,), (1,)), ((), ()))


def from_partner(value, axis, bit):
    mask = 2**bit
    pairs = [(source, source ^ mask) for source in range(lax.axis_size(axis))]
    return lax.ppermute(value, axis, pairs)


def routed_plan(cotangent, expert_ids, gate_probs, saved_gate, saved_up, w_gate, w_up, w_down):
    n_group = lax.axis_size("group")
    n_expert = lax.axis_size("expert")
    tok_rows, model_width = cotangent.shape
    pick_count = expert_ids.shape[2]
    experts = n_group * n_expert // 2
    half_width = model_width // 2
    capacity = saved_gate.shape[1] // (n_group * n_expert)
    assigned = tok_rows * pick_count
    flat_ids = expert_ids.reshape(assigned)
    positions = jnp.arange(assigned, dtype=jnp.int32)
    same_expert = (flat_ids[:, None] == flat_ids[None, :]) & (
        positions[None, :] < positions[:, None]
    )
    slot_pos = jnp.sum(same_expert.astype(jnp.int32), axis=1)
    target = flat_ids * capacity + slot_pos
    places = jnp.arange(experts * capacity, dtype=jnp.int32)
    dispatch_map = (places[:, None] == target[None, :]).astype(jnp.bfloat16)
    scaled = (gate_probs[0][:, :, None] * cotangent[:, None, :].astype(jnp.float32)).astype(
        jnp.bfloat16
    )
    scaled = scaled.reshape(assigned, model_width)
    packed = jnp.dot(dispatch_map, scaled, preferred_element_type=jnp.float32).astype(jnp.bfloat16)
    packed = packed.reshape(n_group // 2, n_expert, capacity, 2, half_width)
    packed = packed.transpose(0, 3, 1, 2, 4).reshape(n_group, n_expert, capacity, half_width)
    arrived = lax.all_to_all(
        lax.all_to_all(packed, "expert", split_axis=1, concat_axis=1, tiled=True),
        "group",
        split_axis=0,
        concat_axis=0,
        tiled=True,
    )
    partner = from_partner(arrived, "group", 0)
    low_half = lax.axis_index("group") % 2 == 0
    front_half = jnp.where(low_half, arrived, partner)
    back_half = jnp.where(low_half, partner, arrived)
    dy_slots = jnp.concatenate([front_half, back_half], axis=3).reshape(-1, model_width)
    pre_gate = saved_gate[0].astype(jnp.float32)
    pre_up = saved_up[0].astype(jnp.float32)
    sigmoid_gate = jax.nn.sigmoid(pre_gate)
    silu_gate = pre_gate * sigmoid_gate
    activation = (silu_gate * pre_up).astype(jnp.bfloat16)
    d_act = lax.dot_general(
        dy_slots, w_down[0], (((1,), (1,)), ((), ())), preferred_element_type=jnp.float32
    )
    d_gate = (d_act * pre_up * sigmoid_gate * (1.0 + pre_gate * (1.0 - sigmoid_gate))).astype(
        jnp.bfloat16
    )
    d_up = (d_act * silu_gate).astype(jnp.bfloat16)
    partial_value = lax.dot_general(
        d_gate, w_gate[0], (((1,), (1,)), ((), ())), preferred_element_type=jnp.float32
    )
    partial_value = partial_value + lax.dot_general(
        d_up, w_up[0], (((1,), (1,)), ((), ())), preferred_element_type=jnp.float32
    )
    partial_value = partial_value.astype(jnp.bfloat16)
    own_half = jnp.where(low_half, partial_value[:, :half_width], partial_value[:, half_width:])
    peer_half = jnp.where(low_half, partial_value[:, half_width:], partial_value[:, :half_width])
    received = from_partner(peer_half, "group", 0)
    combined = (own_half.astype(jnp.float32) + received.astype(jnp.float32)).astype(jnp.bfloat16)
    combined = combined.reshape(n_group, n_expert, capacity, half_width)
    grad_terms = lax.dot_general(
        activation, dy_slots, (((0,), (0,)), ((), ())), preferred_element_type=jnp.float32
    )
    returned = lax.all_to_all(
        lax.all_to_all(combined, "group", split_axis=0, concat_axis=0, tiled=True),
        "expert",
        split_axis=1,
        concat_axis=1,
        tiled=True,
    )
    home_rows = returned.reshape(n_group // 2, 2, n_expert, capacity, half_width)
    home_rows = home_rows.transpose(0, 2, 3, 1, 4).reshape(experts * capacity, model_width)
    per_assign = lax.dot_general(
        dispatch_map, home_rows, (((0,), (0,)), ((), ())), preferred_element_type=jnp.float32
    )
    home_sum = jnp.sum(per_assign.reshape(tok_rows, pick_count, model_width), axis=1)
    grad_down, grad_input = (
        lax.psum_scatter(grad_terms, "replica", scatter_dimension=1, tiled=True),
        lax.psum_scatter(home_sum, "replica", scatter_dimension=1, tiled=True),
    )
    return (grad_input.astype(jnp.bfloat16), grad_down[None])


SCHEDULE = (
    ("zo", 3, 0), ("own", 0, 0), ("saved",), ("zo", 1, 1), ("own", 0, 1), ("metaz",),
    ("meta", 0), ("zo", 3, 1), ("fwa", 0, 0), ("fwb", 0, 0), ("own", 3, 0), ("raw", "x"),
    ("fwa", 0, 1), ("fwb", 0, 1), ("fac", 0), ("own", 1, 1), ("own", 3, 1), ("own", 2, 0),
    ("fwa", 3, 0), ("meta", 1), ("meta", 3), ("zo", 1, 0), ("hid", 0), ("raw", "d"),
    ("meta", 2), ("fwb", 3, 0), ("fwb", 3, 1), ("fwa", 3, 1), ("par", 0, 1), ("own", 2, 1),
    ("raw", "y"), ("par", 0, 0), ("fwa", 1, 1), ("fwb", 2, 0), ("fwb", 1, 1), ("fwa", 2, 0),
    ("fac", 1), ("fac", 3), ("hid", 3), ("par", 3, 1), ("fwb", 2, 1), ("fwa", 2, 1),
    ("par", 3, 0), ("hid", 1), ("par", 1, 0), ("par", 1, 1), ("fac", 2), ("rs2", 3, 1),
    ("hid", 2), ("par", 2, 1), ("rs2", 3, 0), ("par", 2, 0), ("rs1", 0, 1), ("rs3", 3, 1),
    ("rs2", 2, 1), ("grad", 0), ("rs2", 1, 1), ("rs3", 3, 0), ("mrg", 0), ("grad", 1),
    ("mrg", 1), ("rs2", 2, 0), ("rs2", 0, 1), ("rs3", 2, 1), ("rs3", 1, 1), ("grad", 2),
    ("rs2", 0, 0), ("rs3", 2, 0), ("grad", 3), ("rs3", 0, 1), ("drain",), ("rs3", 0, 0),
    ("corner",),
)


def dense_kernel(
    n_group,
    n_expert,
    cot_hbm,
    ids_hbm,
    prob_hbm,
    sg_hbm,
    su_hbm,
    wg_hbm,
    wu_hbm,
    wd_hbm,
    out_ref,
    gd_ref,
    ids_ref,
    prob_ref,
    sg_all,
    su_all,
    wg_ref,
    wu_ref,
    wd_ref,
    cot_all,
    meta_own,
    meta_give,
    meta_take,
    meta_z,
    meta_all,
    act_all,
    f_gate,
    f_up,
    p_buf,
    own0,
    rawr,
    r1,
    s2,
    r2,
    zs,
    zr,
    sibr,
    gt_send,
    gt_recv,
    ssem,
    rsem,
    lsem,
):
    tok, width = cot_hbm.shape
    ht = tok // 2
    half = width // 2
    front, back = pl.ds(0, half // 2), pl.ds(half // 2, half // 2)
    rows_g = n_expert * ht
    slots_g = n_expert * tok
    picks = ids_ref.shape[0]
    experts = meta_own.shape[0]
    f32, bf16 = jnp.float32, jnp.bfloat16
    g = lax.axis_index("group")
    ex = lax.axis_index("expert")
    r = lax.axis_index("replica")
    x, y = ex % 2, ex // 2
    nx, ny = 1 - x, 1 - y
    ex_x, ex_y, ex_d = y * 2 + nx, ny * 2 + x, ny * 2 + nx
    x_dev, y_dev, d_dev = (g, ex_x, r), (g, ex_y, r), (g, ex_d, r)
    sib_dev = (g, ex, 1 - r)

    def group_at(i):
        low = (g % 2 + i % 2) % 2
        high = (g // 2 + i // 2) % 2
        return low + 2 * high

    def z_dev(i, core=None):
        return (group_at(i), ex, r if core is None else core)

    number = {}
    started, arrived, present = [], set(), set()

    def copy(key, src, dst, dev):
        k = number.setdefault(key, len(number))
        return pltpu.make_async_remote_copy(
            src_ref=src,
            dst_ref=dst,
            send_sem=ssem.at[k],
            recv_sem=rsem.at[k],
            device_id=dev,
            device_id_type=MESH,
        )

    def send(key, src, dst, dev):
        one = copy(key, src, dst, dev)
        one.start()
        started.append(one)

    def recv(key, land):
        if key not in arrived:
            arrived.add(key)
            copy(key, land, land, sib_dev).wait_recv()

    def loaded(*which):
        for k in which:
            if k not in present:
                present.add(k)
                loads[k].wait()

    def block(q, e, col, size):
        return cot_all.at[
            pl.ds(pl.multiple_of((q * n_expert + e) * ht, ht), ht), pl.ds(col, size)
        ]

    barrier = pltpu.get_barrier_semaphore()
    peers = [z_dev(i, core) for i in range(1, n_group) for core in (r, 1 - r)]
    peers += [x_dev, y_dev, d_dev, sib_dev]
    for dev in peers:
        pl.semaphore_signal(barrier, inc=1, device_id=dev, device_id_type=MESH)

    routing = [
        pltpu.make_async_copy(ids_hbm, ids_ref, lsem.at[6]),
        pltpu.make_async_copy(prob_hbm, prob_ref, lsem.at[7]),
    ]
    for load in routing:
        load.start()
    place = pltpu.make_async_copy(
        cot_hbm.at[pl.ds(pl.multiple_of(r * ht, ht), ht), :], block(g, ex, 0, width), lsem.at[0]
    )
    place.start()
    loads = [
        pltpu.make_async_copy(src, dst, lsem.at[1 + k])
        for k, (src, dst) in enumerate(
            [
                (sg_hbm.at[0], sg_all.at[r]),
                (su_hbm.at[0], su_all.at[r]),
                (wd_hbm.at[0], wd_ref),
                (wg_hbm.at[0], wg_ref),
                (wu_hbm.at[0], wu_ref),
            ]
        )
    ]
    for load in loads:
        load.start()

    for load in routing:
        load.wait()
    named_by = lax.broadcasted_iota(jnp.int32, (experts, tok), 0)
    named = jnp.zeros((experts, tok), f32)
    weight = jnp.zeros((experts, tok), f32)
    for k in range(picks):
        same = ids_ref[k : k + 1, :] == named_by
        named = named + jnp.where(same, 1.0, 0.0)
        weight = weight + jnp.where(same, prob_ref[k : k + 1, :], 0.0)
    before = lax.broadcasted_iota(jnp.int32, (tok, tok), 0) < lax.broadcasted_iota(
        jnp.int32, (tok, tok), 1
    )
    slot = jnp.dot(
        named.astype(bf16), jnp.where(before, 1.0, 0.0).astype(bf16), preferred_element_type=f32
    )
    slot = jnp.where(named > 0.5, slot, -1.0)
    low_part = jnp.concatenate([slot[:, :ht], weight[:, :ht]], axis=1)
    high_part = jnp.concatenate([slot[:, ht:], weight[:, ht:]], axis=1)
    keep = jnp.where(r == 0, low_part, high_part)
    give = jnp.where(r == 0, high_part, low_part)
    blank = jnp.zeros((experts, tok), f32)

    def in_lanes(part):
        return jnp.concatenate(
            [jnp.where(r == 0, part, blank), jnp.where(r == 0, blank, part)], axis=1
        )

    keep, give = in_lanes(keep), in_lanes(give)
    for e in range(experts):
        meta_give[e] = give[e : e + 1, :]
    place.wait()
    pl.semaphore_wait(barrier, len(peers))

    def ag_cols(h):
        first, size = h * half, half // 2
        return (first, size), (first + size, size)

    def own(i, h):
        if i > 0:
            land_z(i, h)
        if i == 3:
            there = block(group_at(3), ex, h * half, half)
            send(("z", 2, h), there, there, z_dev(1))
        mine = wide_block(i, ex, h)
        send(("x", i, h), mine, mine, x_dev)
        send(("y", i, h), mine, mine, y_dev)

    def wide_block(i, e, h):
        return block(group_at(i), e, h * half, half)

    def land_z(i, h):
        recv(("z", i, h), block(group_at(i), ex, h * half, half))

    def land(name, i, h):
        if name in ("x", "y"):
            recv((name, i, h), wide_block(i, ex_x if name == "x" else ex_y, h))
        else:
            a, b = ag_cols(h)
            recv((name, i, h), block(group_at(i), ex_d, *(a if name == "fa" else b)))

    def fwa(i, h):
        land("x", i, h)
        there = block(group_at(i), ex_x, *ag_cols(h)[0])
        send(("fa", i, h), there, there, y_dev)

    def fwb(i, h):
        land("y", i, h)
        there = block(group_at(i), ex_y, *ag_cols(h)[1])
        send(("fb", i, h), there, there, x_dev)

    def raw(name):
        for part in ("fa", "fb") if name == "d" else (name,):
            land(part, 0, 0)
        there = wide_block(0, {"x": ex_x, "y": ex_y, "d": ex_d}[name], 0)
        send(("raw", name), there, there, z_dev(1))

    def chunk_here(i):
        for h in range(2):
            if i > 0:
                land_z(i, h)
            if (i, h) == (1, 0):
                for e, name in ((ex_x, "x"), (ex_y, "y"), (ex_d, "d")):
                    recv(("raw", name), wide_block(1, e, 0))
                continue
            for name in ("x", "y", "fa", "fb"):
                land(name, i, h)

    def z_out(i, h):
        mine = block(g, ex, h * half, half)
        send(("z", i, h), mine, mine, z_dev(i))

    def experts_of(plane):
        return pl.ds((plane // 2) * n_expert, n_expert)

    def metaz():
        recv(("give",), meta_take)
        for e in range(experts):
            meta_own[e] = keep[e : e + 1, :] + meta_take[e]
        for i in (3, 1, 2):
            send(("mz", i), meta_own.at[experts_of(group_at(i))], meta_z.at[i], z_dev(i))
        meta_z[0] = meta_own[experts_of(g)]

    def meta(i):
        if i > 0:
            recv(("mz", i), meta_z.at[i])
        for key, e, dev in (("mx", ex_x, x_dev), ("my", ex_y, y_dev), ("md", ex_d, d_dev)):
            send((key, i), meta_z.at[i, e], meta_all.at[i, ex], dev)

    def saved():
        send(("sg",), sg_hbm.at[0], sg_all.at[r], sib_dev)
        send(("su",), su_hbm.at[0], su_all.at[r], sib_dev)

    eye = lax.broadcasted_iota(jnp.int32, (2 * tok, 2 * tok), 0) == lax.broadcasted_iota(
        jnp.int32, (2 * tok, 2 * tok), 1
    )
    place_lane = lax.broadcasted_iota(jnp.int32, (ht, slots_g), 1).astype(f32)

    def rows_of(i):
        return pl.ds(pl.multiple_of(group_at(i) * rows_g, rows_g), rows_g)

    def factors(i):
        loaded(0, 1)
        recv(("sg",), sg_all.at[1 - r])
        recv(("su",), su_all.at[1 - r])
        for key, e in (("mx", ex_x), ("my", ex_y), ("md", ex_d)):
            recv((key, i), meta_all.at[i, e])
        meta_all[i, ex] = meta_z[i, ex]
        columns = []
        for b in range(n_expert):
            columns.append(jnp.sum(jnp.where(eye, meta_all[i, b], 0.0), axis=1, keepdims=True))
        slots = pl.ds(pl.multiple_of(group_at(i) * slots_g, slots_g), slots_g)
        to_gate = to_up = to_act = None
        for rho in range(2):
            picked, weights = [], []
            for b in range(n_expert):
                spot = columns[b][rho * tok : rho * tok + ht]
                spot = jnp.where(spot < -0.5, -1.0, spot + float(b * tok))
                picked.append(jnp.where(place_lane == spot, 1.0, 0.0))
                weights.append(columns[b][rho * tok + ht : (rho + 1) * tok])
            select = jnp.concatenate(picked, axis=0).astype(bf16)
            weights = jnp.concatenate(weights, axis=0)
            gate = jnp.dot(select, sg_all[rho, slots, :], preferred_element_type=f32)
            up = jnp.dot(select, su_all[rho, slots, :], preferred_element_type=f32)
            sig = jax.nn.sigmoid(gate)
            silu = gate * sig
            of_up = weights * silu
            of_act = of_up * up
            of_gate = weights * up * sig * (1.0 + gate * (1.0 - sig))
            to_gate = of_gate if rho == 0 else to_gate + of_gate
            to_up = of_up if rho == 0 else to_up + of_up
            to_act = of_act if rho == 0 else to_act + of_act
        f_gate[i] = to_gate
        f_up[i] = to_up
        act_all[rows_of(i), :] = to_act.astype(bf16)

    grads = []

    def hidden(i):
        chunk_here(i)
        loaded(2)
        d_act = lax.dot_general(
            cot_all[rows_of(i), :], wd_ref[...], NT, preferred_element_type=f32
        )
        grads[:] = [(d_act * f_gate[i]).astype(bf16), (d_act * f_up[i]).astype(bf16)]

    def partial(i, f):
        loaded(3, 4)
        first = (1 - r if f == 0 else r) * half
        wide = pl.ds(pl.multiple_of(first, half), half)
        value = lax.dot_general(grads[0], wg_ref[wide, :], NT, preferred_element_type=f32)
        value = value + lax.dot_general(
            grads[1], wu_ref[wide, :], NT, preferred_element_type=f32
        )
        value = value.reshape(2, 2, ht, half)
        if (i, f) == (0, 0):
            own0[...] = value
            return
        p_buf[i, f] = value.astype(bf16)
        if (i, f) == (1, 0):
            for part in (front, back):
                send(
                    ("merge", part is back),
                    p_buf.at[1, 0, :, :, :, part],
                    rawr.at[:, :, :, part],
                    z_dev(1),
                )
        elif i > 0:
            rs_first(i, f)

    def merge(c):
        part = back if c else front
        recv(("merge", bool(c)), rawr.at[:, :, :, part])
        value = own0[:, :, :, part] + rawr[:, :, :, part].astype(f32)
        p_buf[0, 0, :, :, :, part] = value.astype(bf16)
        if c:
            rs_first_b(0, 0)
        else:
            rs_first_a(0, 0)

    def corner():
        send(("corner",), zs.at[0, 0], sibr, sib_dev)

    def rs_first_a(i, f):
        send(("a1", i, f), p_buf.at[i, f, ny, :, :, front], r1.at[i, f, :, :, front], y_dev)

    def rs_first_b(i, f):
        send(("b1", i, f), p_buf.at[i, f, :, nx, :, back], r1.at[i, f, :, :, back], x_dev)

    def rs_first(i, f):
        rs_first_a(i, f)
        rs_first_b(i, f)

    def rs_second(i, f):
        recv(("a1", i, f), r1.at[i, f, :, :, front])
        left = p_buf[i, f, y, :, :, front].astype(f32) + r1[i, f, :, :, front].astype(f32)
        s2[i, f, :, :, front] = left.astype(bf16)
        send(("a2", i, f), s2.at[i, f, nx, :, front], r2.at[i, f, :, front], x_dev)
        recv(("b1", i, f), r1.at[i, f, :, :, back])
        right = p_buf[i, f, :, x, :, back].astype(f32) + r1[i, f, :, :, back].astype(f32)
        s2[i, f, :, :, back] = right.astype(bf16)
        send(("b2", i, f), s2.at[i, f, ny, :, back], r2.at[i, f, :, back], y_dev)

    def rs_third(i, f):
        recv(("a2", i, f), r2.at[i, f, :, front])
        left = s2[i, f, x, :, front].astype(f32) + r2[i, f, :, front].astype(f32)
        zs[i, f, :, front] = left.astype(bf16)
        recv(("b2", i, f), r2.at[i, f, :, back])
        right = s2[i, f, y, :, back].astype(f32) + r2[i, f, :, back].astype(f32)
        zs[i, f, :, back] = right.astype(bf16)
        if i > 0:
            send(("home", i, f), zs.at[i, f], zr.at[i, f], z_dev(i, 1 - r if f == 0 else r))

    def grad_chunk(j):
        base = (1 - r if j < 2 else r) * half + (j % 2) * (half // 2)
        cols = pl.ds(pl.multiple_of(base, half // 2), half // 2)
        value = lax.dot_general(
            act_all[...], cot_all[:, cols], (((0,), (0,)), ((), ())), preferred_element_type=f32
        )
        part = pl.ds((j % 2) * (half // 2), half // 2)
        if j < 2:
            gt_send[:, part] = value.astype(bf16)
        else:
            recv(("grad",), gt_recv)
            gd_ref[:, part] = value + gt_recv[:, part].astype(f32)
        if j == 1:
            send(("grad",), gt_send, gt_recv, sib_dev)

    def drain():
        while started:
            started.pop(0).wait_send()

    steps = {
        "zo": z_out,
        "own": own,
        "fwa": fwa,
        "fwb": fwb,
        "raw": raw,
        "metaz": metaz,
        "meta": meta,
        "saved": saved,
        "fac": factors,
        "hid": hidden,
        "par": partial,
        "rs1": rs_first,
        "mrg": merge,
        "rs2": rs_second,
        "rs3": rs_third,
        "corner": corner,
        "drain": drain,
        "grad": grad_chunk,
    }
    send(("give",), meta_give, meta_take, sib_dev)
    for name, *where in SCHEDULE:
        steps[name](*where)

    def finish(own, f, rows):
        near = (3, 2) if f == 0 else (3, 1, 2)
        for i in near:
            recv(("home", i, f), zr.at[i, f])
        if f == 0:
            recv(("corner",), sibr)
        total = own[...].astype(f32)
        for i in near:
            total = total + zr[i, f].astype(f32)
        out_ref[rows, :] = total.astype(bf16)

    finish(zs.at[0, 1], 1, pl.ds(pl.multiple_of(r * ht, ht), ht))
    finish(sibr, 0, pl.ds(pl.multiple_of((1 - r) * ht, ht), ht))
    drain()


def finish_kernel(rows_ref, down_ref, out_hbm, gd_hbm, sems):
    rows = down_ref.shape[0] // 2
    copies = [pltpu.make_async_copy(rows_ref, out_hbm, sems.at[2])]
    for k in range(2):
        part = pl.ds(k * rows, rows)
        copies.append(
            pltpu.make_async_copy(down_ref.at[part, :], gd_hbm.at[0, part, :], sems.at[k])
        )
    for copy in copies:
        copy.start()
    for copy in copies:
        copy.wait()


def dense_plan(cotangent, expert_ids, gate_probs, saved_gate, saved_up, w_gate, w_up, w_down):
    n_group = lax.axis_size("group")
    n_expert = lax.axis_size("expert")
    tok, width = cotangent.shape
    half = width // 2
    hidden = w_down.shape[1]
    experts = n_group * n_expert // 2
    blocks = n_group * n_expert
    rows_g = n_expert * tok // 2
    bf16, f32 = jnp.bfloat16, jnp.float32
    vmem = pl.BlockSpec(memory_space=pltpu.VMEM)
    ht = tok // 2
    copies = 96
    cotangent, saved_gate, saved_up, w_gate, w_up, w_down = (
        pltpu.with_memory_space_constraint(value, pltpu.HBM)
        for value in (cotangent, saved_gate, saved_up, w_gate, w_up, w_down)
    )
    ids, probs = (
        pltpu.with_memory_space_constraint(value[0].T, pltpu.HBM)
        for value in (expert_ids, gate_probs)
    )
    here = pl.BlockSpec(memory_space=pltpu.HBM)
    rows, down = pl.pallas_call(
        functools.partial(dense_kernel, n_group, n_expert),
        out_shape=(
            jax.ShapeDtypeStruct((tok, half), bf16),
            jax.ShapeDtypeStruct((hidden, half), f32),
        ),
        in_specs=[here] * 8,
        out_specs=(vmem, vmem),
        scratch_shapes=[
            pltpu.VMEM(ids.shape, jnp.int32),
            pltpu.VMEM(probs.shape, f32),
            pltpu.VMEM((2,) + saved_gate.shape[1:], bf16),
            pltpu.VMEM((2,) + saved_up.shape[1:], bf16),
            pltpu.VMEM(w_gate.shape[1:], bf16),
            pltpu.VMEM(w_up.shape[1:], bf16),
            pltpu.VMEM(w_down.shape[1:], bf16),
            pltpu.VMEM((blocks * ht, width), bf16),
            pltpu.VMEM((experts, 1, 2 * tok), f32),
            pltpu.VMEM((experts, 1, 2 * tok), f32),
            pltpu.VMEM((experts, 1, 2 * tok), f32),
            pltpu.VMEM((n_group, n_expert, 1, 2 * tok), f32),
            pltpu.VMEM((n_group, n_expert, 1, 2 * tok), f32),
            pltpu.VMEM((blocks * ht, hidden), bf16),
            pltpu.VMEM((n_group, rows_g, hidden), f32),
            pltpu.VMEM((n_group, rows_g, hidden), f32),
            pltpu.VMEM((n_group, 2, 2, 2, ht, half), bf16),
            pltpu.VMEM((2, 2, ht, half), f32),
            pltpu.VMEM((2, 2, ht, half), bf16),
            pltpu.VMEM((n_group, 2, 2, ht, half), bf16),
            pltpu.VMEM((n_group, 2, 2, ht, half), bf16),
            pltpu.VMEM((n_group, 2, ht, half), bf16),
            pltpu.VMEM((n_group, 2, ht, half), bf16),
            pltpu.VMEM((n_group, 2, ht, half), bf16),
            pltpu.VMEM((ht, half), bf16),
            pltpu.VMEM((hidden, half), bf16),
            pltpu.VMEM((hidden, half), bf16),
            pltpu.SemaphoreType.DMA((copies,)),
            pltpu.SemaphoreType.DMA((copies,)),
            pltpu.SemaphoreType.DMA((8,)),
        ],
        compiler_params=pltpu.CompilerParams(
            collective_id=0, has_side_effects=True, vmem_limit_bytes=40 * 1024 * 1024
        ),
    )(
        cotangent,
        ids,
        probs,
        saved_gate,
        saved_up,
        w_gate,
        w_up,
        w_down,
    )
    return pl.pallas_call(
        finish_kernel,
        out_shape=(
            jax.ShapeDtypeStruct((tok, half), bf16),
            jax.ShapeDtypeStruct((1, hidden, half), f32),
        ),
        in_specs=[vmem] * 2,
        out_specs=(here, here),
        scratch_shapes=[pltpu.SemaphoreType.DMA((3,))],
        compiler_params=pltpu.CompilerParams(vmem_limit_bytes=8 * 1024 * 1024),
    )(rows, down)


def on_device(cotangent, expert_ids, gate_probs, saved_gate, saved_up, w_gate, w_up, w_down):
    n_group = lax.axis_size("group")
    n_expert = lax.axis_size("expert")
    n_replica = lax.axis_size("replica")
    tok_rows = cotangent.shape[0]
    capacity = saved_gate.shape[1] // (n_group * n_expert)
    small = n_group == 4 and n_expert == 4 and n_replica == 2
    plan = routed_plan
    if small and capacity == tok_rows and 2 * tok_rows == 128:
        plan = dense_plan
    return plan(cotangent, expert_ids, gate_probs, saved_gate, saved_up, w_gate, w_up, w_down)


def solution(mesh):
    return jax.shard_map(
        on_device,
        mesh=mesh,
        in_specs=(
            P(("group", "expert"), None),
            P("replica", ("group", "expert"), None),
            P("replica", ("group", "expert"), None),
            P(("group", "expert"), "replica", None),
            P(("group", "expert"), "replica", None),
            P(("group", "expert"), None, None),
            P(("group", "expert"), None, None),
            P(("group", "expert"), None, None),
        ),
        out_specs=(P(("group", "expert"), "replica"), P(("group", "expert"), None, "replica")),
        check_vma=False,
    )
```

```python
import functools

import jax
import jax.numpy as jnp
from jax import lax
from jax.experimental import pallas as pl
from jax.experimental.pallas import tpu as pltpu
from jax.sharding import PartitionSpec as P

MESH = pl.DeviceIdType.MESH
NT = (((1,), (1,)), ((), ()))


def from_partner(value, axis, bit):
    mask = 2**bit
    pairs = [(source, source ^ mask) for source in range(lax.axis_size(axis))]
    return lax.ppermute(value, axis, pairs)


def routed_plan(cotangent, expert_ids, gate_probs, saved_gate, saved_up, w_gate, w_up, w_down):
    n_group = lax.axis_size("group")
    n_expert = lax.axis_size("expert")
    tok_rows, model_width = cotangent.shape
    pick_count = expert_ids.shape[2]
    experts = n_group * n_expert // 2
    half_width = model_width // 2
    capacity = saved_gate.shape[1] // (n_group * n_expert)
    assigned = tok_rows * pick_count
    flat_ids = expert_ids.reshape(assigned)
    positions = jnp.arange(assigned, dtype=jnp.int32)
    same_expert = (flat_ids[:, None] == flat_ids[None, :]) & (
        positions[None, :] < positions[:, None]
    )
    slot_pos = jnp.sum(same_expert.astype(jnp.int32), axis=1)
    target = flat_ids * capacity + slot_pos
    places = jnp.arange(experts * capacity, dtype=jnp.int32)
    dispatch_map = (places[:, None] == target[None, :]).astype(jnp.bfloat16)
    scaled = (gate_probs[0][:, :, None] * cotangent[:, None, :].astype(jnp.float32)).astype(
        jnp.bfloat16
    )
    scaled = scaled.reshape(assigned, model_width)
    packed = jnp.dot(dispatch_map, scaled, preferred_element_type=jnp.float32).astype(jnp.bfloat16)
    packed = packed.reshape(n_group // 2, n_expert, capacity, 2, half_width)
    packed = packed.transpose(0, 3, 1, 2, 4).reshape(n_group, n_expert, capacity, half_width)
    arrived = lax.all_to_all(
        lax.all_to_all(packed, "expert", split_axis=1, concat_axis=1, tiled=True),
        "group",
        split_axis=0,
        concat_axis=0,
        tiled=True,
    )
    partner = from_partner(arrived, "group", 0)
    low_half = lax.axis_index("group") % 2 == 0
    front_half = jnp.where(low_half, arrived, partner)
    back_half = jnp.where(low_half, partner, arrived)
    dy_slots = jnp.concatenate([front_half, back_half], axis=3).reshape(-1, model_width)
    pre_gate = saved_gate[0].astype(jnp.float32)
    pre_up = saved_up[0].astype(jnp.float32)
    sigmoid_gate = jax.nn.sigmoid(pre_gate)
    silu_gate = pre_gate * sigmoid_gate
    activation = (silu_gate * pre_up).astype(jnp.bfloat16)
    d_act = lax.dot_general(
        dy_slots, w_down[0], (((1,), (1,)), ((), ())), preferred_element_type=jnp.float32
    )
    d_gate = (d_act * pre_up * sigmoid_gate * (1.0 + pre_gate * (1.0 - sigmoid_gate))).astype(
        jnp.bfloat16
    )
    d_up = (d_act * silu_gate).astype(jnp.bfloat16)
    partial_value = lax.dot_general(
        d_gate, w_gate[0], (((1,), (1,)), ((), ())), preferred_element_type=jnp.float32
    )
    partial_value = partial_value + lax.dot_general(
        d_up, w_up[0], (((1,), (1,)), ((), ())), preferred_element_type=jnp.float32
    )
    partial_value = partial_value.astype(jnp.bfloat16)
    own_half = jnp.where(low_half, partial_value[:, :half_width], partial_value[:, half_width:])
    peer_half = jnp.where(low_half, partial_value[:, half_width:], partial_value[:, :half_width])
    received = from_partner(peer_half, "group", 0)
    combined = (own_half.astype(jnp.float32) + received.astype(jnp.float32)).astype(jnp.bfloat16)
    combined = combined.reshape(n_group, n_expert, capacity, half_width)
    grad_terms = lax.dot_general(
        activation, dy_slots, (((0,), (0,)), ((), ())), preferred_element_type=jnp.float32
    )
    returned = lax.all_to_all(
        lax.all_to_all(combined, "group", split_axis=0, concat_axis=0, tiled=True),
        "expert",
        split_axis=1,
        concat_axis=1,
        tiled=True,
    )
    home_rows = returned.reshape(n_group // 2, 2, n_expert, capacity, half_width)
    home_rows = home_rows.transpose(0, 2, 3, 1, 4).reshape(experts * capacity, model_width)
    per_assign = lax.dot_general(
        dispatch_map, home_rows, (((0,), (0,)), ((), ())), preferred_element_type=jnp.float32
    )
    home_sum = jnp.sum(per_assign.reshape(tok_rows, pick_count, model_width), axis=1)
    grad_down, grad_input = (
        lax.psum_scatter(grad_terms, "replica", scatter_dimension=1, tiled=True),
        lax.psum_scatter(home_sum, "replica", scatter_dimension=1, tiled=True),
    )
    return (grad_input.astype(jnp.bfloat16), grad_down[None])


SCHEDULE = (
    ("zo", 3, 0), ("own", 0, 0), ("saved",), ("zo", 1, 1), ("own", 0, 1), ("metaz",),
    ("meta", 0), ("zo", 3, 1), ("fwa", 0, 0), ("fwb", 0, 0), ("own", 3, 0), ("raw", "x"),
    ("fwa", 0, 1), ("fwb", 0, 1), ("fac", 0), ("own", 1, 1), ("own", 3, 1), ("own", 2, 0),
    ("fwa", 3, 0), ("meta", 1), ("meta", 3), ("zo", 1, 0), ("hid", 0), ("raw", "d"),
    ("meta", 2), ("fwb", 3, 0), ("fwb", 3, 1), ("fwa", 3, 1), ("par", 0, 1), ("own", 2, 1),
    ("raw", "y"), ("par", 0, 0), ("fwa", 1, 1), ("fwb", 2, 0), ("fwb", 1, 1), ("fwa", 2, 0),
    ("fac", 1), ("fac", 3), ("hid", 3), ("par", 3, 1), ("fwb", 2, 1), ("fwa", 2, 1),
    ("par", 3, 0), ("hid", 1), ("par", 1, 0), ("par", 1, 1), ("fac", 2), ("rs2", 3, 1),
    ("hid", 2), ("par", 2, 1), ("rs2", 3, 0), ("par", 2, 0), ("rs1", 0, 1), ("rs3", 3, 1),
    ("rs2", 2, 1), ("grad", 0), ("rs2", 1, 1), ("rs3", 3, 0), ("mrg", 0), ("mrg", 1),
    ("grad", 1), ("rs2", 2, 0), ("rs2", 0, 1), ("rs3", 2, 1), ("rs3", 1, 1), ("grad", 2),
    ("rs2", 0, 0), ("rs3", 2, 0), ("grad", 3), ("rs3", 0, 1), ("drain",), ("rs3", 0, 0),
    ("corner",),
)


def dense_kernel(
    n_group,
    n_expert,
    cot_hbm,
    ids_hbm,
    prob_hbm,
    sg_hbm,
    su_hbm,
    wg_hbm,
    wu_hbm,
    wd_hbm,
    out_ref,
    gd_ref,
    ids_ref,
    prob_ref,
    sg_all,
    su_all,
    wg_ref,
    wu_ref,
    wd_ref,
    cot_all,
    meta_own,
    meta_give,
    meta_take,
    meta_z,
    meta_all,
    act_all,
    f_gate,
    f_up,
    p_buf,
    own0,
    rawr,
    r1,
    s2,
    r2,
    zs,
    zr,
    sibr,
    gt_send,
    gt_recv,
    ssem,
    rsem,
    lsem,
):
    tok, width = cot_hbm.shape
    ht = tok // 2
    half = width // 2
    front, back = pl.ds(0, half // 2), pl.ds(half // 2, half // 2)
    rows_g = n_expert * ht
    slots_g = n_expert * tok
    picks = ids_ref.shape[0]
    experts = meta_own.shape[0]
    f32, bf16 = jnp.float32, jnp.bfloat16
    g = lax.axis_index("group")
    ex = lax.axis_index("expert")
    r = lax.axis_index("replica")
    x, y = ex % 2, ex // 2
    nx, ny = 1 - x, 1 - y
    ex_x, ex_y, ex_d = y * 2 + nx, ny * 2 + x, ny * 2 + nx
    x_dev, y_dev, d_dev = (g, ex_x, r), (g, ex_y, r), (g, ex_d, r)
    sib_dev = (g, ex, 1 - r)

    def group_at(i):
        low = (g % 2 + i % 2) % 2
        high = (g // 2 + i // 2) % 2
        return low + 2 * high

    def z_dev(i, core=None):
        return (group_at(i), ex, r if core is None else core)

    number = {}
    started, arrived, present = [], set(), set()

    def copy(key, src, dst, dev):
        k = number.setdefault(key, len(number))
        return pltpu.make_async_remote_copy(
            src_ref=src,
            dst_ref=dst,
            send_sem=ssem.at[k],
            recv_sem=rsem.at[k],
            device_id=dev,
            device_id_type=MESH,
        )

    def send(key, src, dst, dev):
        one = copy(key, src, dst, dev)
        one.start()
        started.append(one)

    def recv(key, land):
        if key not in arrived:
            arrived.add(key)
            copy(key, land, land, sib_dev).wait_recv()

    def loaded(*which):
        for k in which:
            if k not in present:
                present.add(k)
                loads[k].wait()

    def block(q, e, col, size):
        return cot_all.at[
            pl.ds(pl.multiple_of((q * n_expert + e) * ht, ht), ht), pl.ds(col, size)
        ]

    barrier = pltpu.get_barrier_semaphore()
    peers = [z_dev(i, core) for i in range(1, n_group) for core in (r, 1 - r)]
    peers += [x_dev, y_dev, d_dev, sib_dev]
    for dev in peers:
        pl.semaphore_signal(barrier, inc=1, device_id=dev, device_id_type=MESH)

    routing = [
        pltpu.make_async_copy(ids_hbm, ids_ref, lsem.at[6]),
        pltpu.make_async_copy(prob_hbm, prob_ref, lsem.at[7]),
    ]
    for load in routing:
        load.start()
    place = pltpu.make_async_copy(
        cot_hbm.at[pl.ds(pl.multiple_of(r * ht, ht), ht), :], block(g, ex, 0, width), lsem.at[0]
    )
    place.start()
    loads = [
        pltpu.make_async_copy(src, dst, lsem.at[1 + k])
        for k, (src, dst) in enumerate(
            [
                (sg_hbm.at[0], sg_all.at[r]),
                (su_hbm.at[0], su_all.at[r]),
                (wd_hbm.at[0], wd_ref),
                (wg_hbm.at[0], wg_ref),
                (wu_hbm.at[0], wu_ref),
            ]
        )
    ]
    for load in loads:
        load.start()

    for load in routing:
        load.wait()
    named_by = lax.broadcasted_iota(jnp.int32, (experts, tok), 0)
    named = jnp.zeros((experts, tok), f32)
    weight = jnp.zeros((experts, tok), f32)
    for k in range(picks):
        same = ids_ref[k : k + 1, :] == named_by
        named = named + jnp.where(same, 1.0, 0.0)
        weight = weight + jnp.where(same, prob_ref[k : k + 1, :], 0.0)
    before = lax.broadcasted_iota(jnp.int32, (tok, tok), 0) < lax.broadcasted_iota(
        jnp.int32, (tok, tok), 1
    )
    slot = jnp.dot(
        named.astype(bf16), jnp.where(before, 1.0, 0.0).astype(bf16), preferred_element_type=f32
    )
    slot = jnp.where(named > 0.5, slot, -1.0)
    low_part = jnp.concatenate([slot[:, :ht], weight[:, :ht]], axis=1)
    high_part = jnp.concatenate([slot[:, ht:], weight[:, ht:]], axis=1)
    keep = jnp.where(r == 0, low_part, high_part)
    give = jnp.where(r == 0, high_part, low_part)
    blank = jnp.zeros((experts, tok), f32)

    def in_lanes(part):
        return jnp.concatenate(
            [jnp.where(r == 0, part, blank), jnp.where(r == 0, blank, part)], axis=1
        )

    keep, give = in_lanes(keep), in_lanes(give)
    for e in range(experts):
        meta_give[e] = give[e : e + 1, :]
    place.wait()
    pl.semaphore_wait(barrier, len(peers))

    def ag_cols(h):
        first, size = h * half, half // 2
        return (first, size), (first + size, size)

    def own(i, h):
        if i > 0:
            land_z(i, h)
        if i == 3:
            there = block(group_at(3), ex, h * half, half)
            send(("z", 2, h), there, there, z_dev(1))
        mine = wide_block(i, ex, h)
        send(("x", i, h), mine, mine, x_dev)
        send(("y", i, h), mine, mine, y_dev)

    def wide_block(i, e, h):
        return block(group_at(i), e, h * half, half)

    def land_z(i, h):
        recv(("z", i, h), block(group_at(i), ex, h * half, half))

    def land(name, i, h):
        if name in ("x", "y"):
            recv((name, i, h), wide_block(i, ex_x if name == "x" else ex_y, h))
        else:
            a, b = ag_cols(h)
            recv((name, i, h), block(group_at(i), ex_d, *(a if name == "fa" else b)))

    def fwa(i, h):
        land("x", i, h)
        there = block(group_at(i), ex_x, *ag_cols(h)[0])
        send(("fa", i, h), there, there, y_dev)

    def fwb(i, h):
        land("y", i, h)
        there = block(group_at(i), ex_y, *ag_cols(h)[1])
        send(("fb", i, h), there, there, x_dev)

    def raw(name):
        for part in ("fa", "fb") if name == "d" else (name,):
            land(part, 0, 0)
        there = wide_block(0, {"x": ex_x, "y": ex_y, "d": ex_d}[name], 0)
        send(("raw", name), there, there, z_dev(1))

    def chunk_here(i):
        for h in range(2):
            if i > 0:
                land_z(i, h)
            if (i, h) == (1, 0):
                for e, name in ((ex_x, "x"), (ex_y, "y"), (ex_d, "d")):
                    recv(("raw", name), wide_block(1, e, 0))
                continue
            for name in ("x", "y", "fa", "fb"):
                land(name, i, h)

    def z_out(i, h):
        mine = block(g, ex, h * half, half)
        send(("z", i, h), mine, mine, z_dev(i))

    def experts_of(plane):
        return pl.ds((plane // 2) * n_expert, n_expert)

    def metaz():
        recv(("give",), meta_take)
        for e in range(experts):
            meta_own[e] = keep[e : e + 1, :] + meta_take[e]
        for i in (3, 1, 2):
            send(("mz", i), meta_own.at[experts_of(group_at(i))], meta_z.at[i], z_dev(i))
        meta_z[0] = meta_own[experts_of(g)]

    def meta(i):
        if i > 0:
            recv(("mz", i), meta_z.at[i])
        for key, e, dev in (("mx", ex_x, x_dev), ("my", ex_y, y_dev), ("md", ex_d, d_dev)):
            send((key, i), meta_z.at[i, e], meta_all.at[i, ex], dev)

    def saved():
        send(("sg",), sg_hbm.at[0], sg_all.at[r], sib_dev)
        send(("su",), su_hbm.at[0], su_all.at[r], sib_dev)

    eye = lax.broadcasted_iota(jnp.int32, (2 * tok, 2 * tok), 0) == lax.broadcasted_iota(
        jnp.int32, (2 * tok, 2 * tok), 1
    )
    place_lane = lax.broadcasted_iota(jnp.int32, (ht, slots_g), 1).astype(f32)

    def rows_of(i):
        return pl.ds(pl.multiple_of(group_at(i) * rows_g, rows_g), rows_g)

    def factors(i):
        loaded(0, 1)
        recv(("sg",), sg_all.at[1 - r])
        recv(("su",), su_all.at[1 - r])
        for key, e in (("mx", ex_x), ("my", ex_y), ("md", ex_d)):
            recv((key, i), meta_all.at[i, e])
        meta_all[i, ex] = meta_z[i, ex]
        columns = []
        for b in range(n_expert):
            columns.append(jnp.sum(jnp.where(eye, meta_all[i, b], 0.0), axis=1, keepdims=True))
        slots = pl.ds(pl.multiple_of(group_at(i) * slots_g, slots_g), slots_g)
        to_gate = to_up = to_act = None
        for rho in range(2):
            picked, weights = [], []
            for b in range(n_expert):
                spot = columns[b][rho * tok : rho * tok + ht]
                spot = jnp.where(spot < -0.5, -1.0, spot + float(b * tok))
                picked.append(jnp.where(place_lane == spot, 1.0, 0.0))
                weights.append(columns[b][rho * tok + ht : (rho + 1) * tok])
            select = jnp.concatenate(picked, axis=0).astype(bf16)
            weights = jnp.concatenate(weights, axis=0)
            gate = jnp.dot(select, sg_all[rho, slots, :], preferred_element_type=f32)
            up = jnp.dot(select, su_all[rho, slots, :], preferred_element_type=f32)
            sig = jax.nn.sigmoid(gate)
            silu = gate * sig
            of_up = weights * silu
            of_act = of_up * up
            of_gate = weights * up * sig * (1.0 + gate * (1.0 - sig))
            to_gate = of_gate if rho == 0 else to_gate + of_gate
            to_up = of_up if rho == 0 else to_up + of_up
            to_act = of_act if rho == 0 else to_act + of_act
        f_gate[i] = to_gate
        f_up[i] = to_up
        act_all[rows_of(i), :] = to_act.astype(bf16)

    grads = []

    def hidden(i):
        chunk_here(i)
        loaded(2)
        d_act = lax.dot_general(
            cot_all[rows_of(i), :], wd_ref[...], NT, preferred_element_type=f32
        )
        grads[:] = [(d_act * f_gate[i]).astype(bf16), (d_act * f_up[i]).astype(bf16)]

    def partial(i, f):
        loaded(3, 4)
        first = (1 - r if f == 0 else r) * half
        wide = pl.ds(pl.multiple_of(first, half), half)
        value = lax.dot_general(grads[0], wg_ref[wide, :], NT, preferred_element_type=f32)
        value = value + lax.dot_general(
            grads[1], wu_ref[wide, :], NT, preferred_element_type=f32
        )
        value = value.reshape(2, 2, ht, half)
        if (i, f) == (0, 0):
            own0[...] = value
            return
        p_buf[i, f] = value.astype(bf16)
        if (i, f) == (1, 0):
            for part in (front, back):
                send(
                    ("merge", part is back),
                    p_buf.at[1, 0, :, :, :, part],
                    rawr.at[:, :, :, part],
                    z_dev(1),
                )
        elif i > 0:
            rs_first(i, f)

    def merge(c):
        part = back if c else front
        recv(("merge", bool(c)), rawr.at[:, :, :, part])
        value = own0[:, :, :, part] + rawr[:, :, :, part].astype(f32)
        p_buf[0, 0, :, :, :, part] = value.astype(bf16)
        if c:
            rs_first_b(0, 0)
        else:
            rs_first_a(0, 0)

    def corner():
        send(("corner",), zs.at[0, 0], sibr, sib_dev)

    def rs_first_a(i, f):
        send(("a1", i, f), p_buf.at[i, f, ny, :, :, front], r1.at[i, f, :, :, front], y_dev)

    def rs_first_b(i, f):
        send(("b1", i, f), p_buf.at[i, f, :, nx, :, back], r1.at[i, f, :, :, back], x_dev)

    def rs_first(i, f):
        rs_first_a(i, f)
        rs_first_b(i, f)

    def rs_second(i, f):
        recv(("a1", i, f), r1.at[i, f, :, :, front])
        left = p_buf[i, f, y, :, :, front].astype(f32) + r1[i, f, :, :, front].astype(f32)
        s2[i, f, :, :, front] = left.astype(bf16)
        send(("a2", i, f), s2.at[i, f, nx, :, front], r2.at[i, f, :, front], x_dev)
        recv(("b1", i, f), r1.at[i, f, :, :, back])
        right = p_buf[i, f, :, x, :, back].astype(f32) + r1[i, f, :, :, back].astype(f32)
        s2[i, f, :, :, back] = right.astype(bf16)
        send(("b2", i, f), s2.at[i, f, ny, :, back], r2.at[i, f, :, back], y_dev)

    def rs_third(i, f):
        recv(("a2", i, f), r2.at[i, f, :, front])
        left = s2[i, f, x, :, front].astype(f32) + r2[i, f, :, front].astype(f32)
        zs[i, f, :, front] = left.astype(bf16)
        recv(("b2", i, f), r2.at[i, f, :, back])
        right = s2[i, f, y, :, back].astype(f32) + r2[i, f, :, back].astype(f32)
        zs[i, f, :, back] = right.astype(bf16)
        if i > 0:
            send(("home", i, f), zs.at[i, f], zr.at[i, f], z_dev(i, 1 - r if f == 0 else r))

    def grad_chunk(j):
        base = (1 - r if j < 2 else r) * half + (j % 2) * (half // 2)
        cols = pl.ds(pl.multiple_of(base, half // 2), half // 2)
        value = lax.dot_general(
            act_all[...], cot_all[:, cols], (((0,), (0,)), ((), ())), preferred_element_type=f32
        )
        part = pl.ds((j % 2) * (half // 2), half // 2)
        if j < 2:
            gt_send[:, part] = value.astype(bf16)
        else:
            recv(("grad",), gt_recv)
            gd_ref[:, part] = value + gt_recv[:, part].astype(f32)
        if j == 1:
            send(("grad",), gt_send, gt_recv, sib_dev)

    def drain():
        while started:
            started.pop(0).wait_send()

    steps = {
        "zo": z_out,
        "own": own,
        "fwa": fwa,
        "fwb": fwb,
        "raw": raw,
        "metaz": metaz,
        "meta": meta,
        "saved": saved,
        "fac": factors,
        "hid": hidden,
        "par": partial,
        "rs1": rs_first,
        "mrg": merge,
        "rs2": rs_second,
        "rs3": rs_third,
        "corner": corner,
        "drain": drain,
        "grad": grad_chunk,
    }
    send(("give",), meta_give, meta_take, sib_dev)
    for name, *where in SCHEDULE:
        steps[name](*where)

    def finish(own, f, rows):
        near = (3, 2) if f == 0 else (3, 1, 2)
        for i in near:
            recv(("home", i, f), zr.at[i, f])
        if f == 0:
            recv(("corner",), sibr)
        total = own[...].astype(f32)
        for i in near:
            total = total + zr[i, f].astype(f32)
        out_ref[rows, :] = total.astype(bf16)

    finish(zs.at[0, 1], 1, pl.ds(pl.multiple_of(r * ht, ht), ht))
    finish(sibr, 0, pl.ds(pl.multiple_of((1 - r) * ht, ht), ht))
    drain()


def finish_kernel(rows_ref, down_ref, out_hbm, gd_hbm, sems):
    rows = down_ref.shape[0] // 2
    copies = [pltpu.make_async_copy(rows_ref, out_hbm, sems.at[2])]
    for k in range(2):
        part = pl.ds(k * rows, rows)
        copies.append(
            pltpu.make_async_copy(down_ref.at[part, :], gd_hbm.at[0, part, :], sems.at[k])
        )
    for copy in copies:
        copy.start()
    for copy in copies:
        copy.wait()


def dense_plan(cotangent, expert_ids, gate_probs, saved_gate, saved_up, w_gate, w_up, w_down):
    n_group = lax.axis_size("group")
    n_expert = lax.axis_size("expert")
    tok, width = cotangent.shape
    half = width // 2
    hidden = w_down.shape[1]
    experts = n_group * n_expert // 2
    blocks = n_group * n_expert
    rows_g = n_expert * tok // 2
    bf16, f32 = jnp.bfloat16, jnp.float32
    vmem = pl.BlockSpec(memory_space=pltpu.VMEM)
    ht = tok // 2
    copies = 96
    cotangent, saved_gate, saved_up, w_gate, w_up, w_down = (
        pltpu.with_memory_space_constraint(value, pltpu.HBM)
        for value in (cotangent, saved_gate, saved_up, w_gate, w_up, w_down)
    )
    ids, probs = (
        pltpu.with_memory_space_constraint(value[0].T, pltpu.HBM)
        for value in (expert_ids, gate_probs)
    )
    here = pl.BlockSpec(memory_space=pltpu.HBM)
    rows, down = pl.pallas_call(
        functools.partial(dense_kernel, n_group, n_expert),
        out_shape=(
            jax.ShapeDtypeStruct((tok, half), bf16),
            jax.ShapeDtypeStruct((hidden, half), f32),
        ),
        in_specs=[here] * 8,
        out_specs=(vmem, vmem),
        scratch_shapes=[
            pltpu.VMEM(ids.shape, jnp.int32),
            pltpu.VMEM(probs.shape, f32),
            pltpu.VMEM((2,) + saved_gate.shape[1:], bf16),
            pltpu.VMEM((2,) + saved_up.shape[1:], bf16),
            pltpu.VMEM(w_gate.shape[1:], bf16),
            pltpu.VMEM(w_up.shape[1:], bf16),
            pltpu.VMEM(w_down.shape[1:], bf16),
            pltpu.VMEM((blocks * ht, width), bf16),
            pltpu.VMEM((experts, 1, 2 * tok), f32),
            pltpu.VMEM((experts, 1, 2 * tok), f32),
            pltpu.VMEM((experts, 1, 2 * tok), f32),
            pltpu.VMEM((n_group, n_expert, 1, 2 * tok), f32),
            pltpu.VMEM((n_group, n_expert, 1, 2 * tok), f32),
            pltpu.VMEM((blocks * ht, hidden), bf16),
            pltpu.VMEM((n_group, rows_g, hidden), f32),
            pltpu.VMEM((n_group, rows_g, hidden), f32),
            pltpu.VMEM((n_group, 2, 2, 2, ht, half), bf16),
            pltpu.VMEM((2, 2, ht, half), f32),
            pltpu.VMEM((2, 2, ht, half), bf16),
            pltpu.VMEM((n_group, 2, 2, ht, half), bf16),
            pltpu.VMEM((n_group, 2, 2, ht, half), bf16),
            pltpu.VMEM((n_group, 2, ht, half), bf16),
            pltpu.VMEM((n_group, 2, ht, half), bf16),
            pltpu.VMEM((n_group, 2, ht, half), bf16),
            pltpu.VMEM((ht, half), bf16),
            pltpu.VMEM((hidden, half), bf16),
            pltpu.VMEM((hidden, half), bf16),
            pltpu.SemaphoreType.DMA((copies,)),
            pltpu.SemaphoreType.DMA((copies,)),
            pltpu.SemaphoreType.DMA((8,)),
        ],
        compiler_params=pltpu.CompilerParams(
            collective_id=0, has_side_effects=True, vmem_limit_bytes=40 * 1024 * 1024
        ),
    )(
        cotangent,
        ids,
        probs,
        saved_gate,
        saved_up,
        w_gate,
        w_up,
        w_down,
    )
    return pl.pallas_call(
        finish_kernel,
        out_shape=(
            jax.ShapeDtypeStruct((tok, half), bf16),
            jax.ShapeDtypeStruct((1, hidden, half), f32),
        ),
        in_specs=[vmem] * 2,
        out_specs=(here, here),
        scratch_shapes=[pltpu.SemaphoreType.DMA((3,))],
        compiler_params=pltpu.CompilerParams(vmem_limit_bytes=8 * 1024 * 1024),
    )(rows, down)


def on_device(cotangent, expert_ids, gate_probs, saved_gate, saved_up, w_gate, w_up, w_down):
    n_group = lax.axis_size("group")
    n_expert = lax.axis_size("expert")
    n_replica = lax.axis_size("replica")
    tok_rows = cotangent.shape[0]
    capacity = saved_gate.shape[1] // (n_group * n_expert)
    small = n_group == 4 and n_expert == 4 and n_replica == 2
    plan = routed_plan
    if small and capacity == tok_rows and 2 * tok_rows == 128:
        plan = dense_plan
    return plan(cotangent, expert_ids, gate_probs, saved_gate, saved_up, w_gate, w_up, w_down)


def solution(mesh):
    return jax.shard_map(
        on_device,
        mesh=mesh,
        in_specs=(
            P(("group", "expert"), None),
            P("replica", ("group", "expert"), None),
            P("replica", ("group", "expert"), None),
            P(("group", "expert"), "replica", None),
            P(("group", "expert"), "replica", None),
            P(("group", "expert"), None, None),
            P(("group", "expert"), None, None),
            P(("group", "expert"), None, None),
        ),
        out_specs=(P(("group", "expert"), "replica"), P(("group", "expert"), None, "replica")),
        check_vma=False,
    )
```
